256 devices in a mesh: pb: 64 (over x, z, core), ka: 4 (over y).
Axes of the slice: x: 4, y: 4, z: 8, core: 2. Of those that a mesh axis runs over, the one named last changes fastest.
Arguments:
- valence: float32 [1664, 64, 1024], P('pb', 'ka'), may hold values from -6 to 6
- conduction: bfloat16 [1664, 196, 1024], P('pb', None, 'ka'), may hold values from -0.0024414062 to 0.0024414062
- screened: float32 [64, 1024, 1024], P('pb'), may hold values from -1 to 3, as said below
- momentum: int32 [1664, 1], P('pb'), may hold values from 0 to 63; in each aligned block of 26 rows (0 to 25, 26 to 51, ...) at most 2 rows name the same one
- kpairs: int32 [1664, 2], P('pb'), may hold values from 0 to 63
- kpoint_slot: int32 [64], replicated, may hold values from 0 to 63, each once
- trial_blocks: float32 [64, 14336], P('pb', 'ka'), may hold values from -6 to 6
Outputs:
- response: float32 [64, 14336], P('pb', 'ka')
The draws below stay inside these ranges and needn't reach their ends.
Inputs may be any that keep to these rules, and one draw needn't show every extreme that they name: Among the k-pairs of one index of pb (rows i * 26 to (i + 1) * 26 - 1), at most 2 share a momentum transfer. `kpoint_slot`: each row number appears once. `screened`: each matrix is symmetric.
All inputs are finite; a program needn't handle non-finite values.
Results may differ from the reference program's by a relative error of at most 0.0003.
Values sent between devices are 32-bit elements; how exact they have to be, the bound alone decides.
No kernel may reach another device: no remote copies, remote signals or barrier semaphores. Data moves between devices by JAX's collectives and lax.ppermute only.
A program may use at most 128 MiB of HBM per device.

```python
import math
import jax
import jax.numpy as jnp
import numpy as np
from jax import lax

NG = 1024
VB = 8
CB = 14
NTRIAL = 128
PAIR_DEV = 26
VP = 64
CP = 196
VC = 112
Q = 64
PAIRS = 1664
NK = 64
CAP = 2


def draw_screened(key, part):
    key_diag = jax.random.fold_in(key, 11)
    key_off = jax.random.fold_in(key, 12)
    diagonal = jnp.exp(jax.random.uniform(key_diag, (Q, NG), jnp.float32, math.log(0.5), math.log(2.0)))
    jitter = jnp.clip(jax.random.normal(key_off, (Q, NG, NG), jnp.float32), -4.0, 4.0)
    symmetric = (jitter + jnp.swapaxes(jitter, 1, 2)) * (0.25 / math.sqrt(NG))
    identity = jnp.eye(NG, dtype=jnp.float32)
    return symmetric + diagonal[:, :, None] * identity[None, :, :]


def touch_ends(array, rng, least, high):
    index_at = [jax.random.randint(jax.random.fold_in(rng, axis), (), 0, length) for axis, length in enumerate(array.shape)]
    longest = array.shape.index(max(array.shape))
    neighbour = index_at[:longest] + [(index_at[longest] + 1) % array.shape[longest]] + index_at[longest + 1:]
    return array.at[tuple(index_at)].set(least).at[tuple(neighbour)].set(high)


def shard_levels(rng, extent, split, least, largest):
    gain, own = 1.0, jax.random.fold_in(rng, 6)
    for position, shards_of in split:
        draws = jnp.exp(jax.random.uniform(jax.random.fold_in(own, position), (shards_of,), jnp.float32, least / len(split), largest / len(split)))
        gain = gain * jnp.repeat(draws, extent[position] // shards_of).reshape([-1 if axis == position else 1 for axis in range(len(extent))])
    return gain


def routed_block(own_key, own, number, rows, number_of, top, most, skew):
    ranking = jax.random.permutation(own_key, number_of)
    crowded, usual = load_shares(number_of, rows * top, most, skew, True), load_shares(number_of, rows * top, most, skew, False)
    places = jnp.arange(number_of)

    def named(sizes, turn):
        used = int((sizes > 0).sum())
        fixed = max(1, used // 4)
        passed = fixed + (places - fixed + turn * (used - fixed)) % max(1, number_of - fixed)
        return jnp.zeros((number_of,), jnp.int32).at[ranking[jnp.where(places < fixed, places, passed)]].set(jnp.asarray(sizes, jnp.int32))

    sizes = jnp.where(number % 4 == 0, named(crowded, number // 4), named(usual, number - number // 4 - 1))
    mixed = jax.random.permutation(jax.random.fold_in(own, 3), number_of)
    donor, taker = mixed[0:number_of // 2 * 2:2], mixed[1:number_of // 2 * 2:2]
    margin = jnp.minimum(sizes[donor] - 1, most - sizes[taker]) // 2
    margin = jnp.where((donor == ranking[0]) | (taker == ranking[0]) | (sizes[taker] == 0), 0, jnp.maximum(margin, 0))
    passed = jax.random.randint(jax.random.fold_in(own, 4), (number_of // 2,), 0, 1 << 20) % (margin + 1)
    sizes = sizes.at[donor].add(-passed).at[taker].add(passed)
    labels = jnp.searchsorted(jnp.cumsum(sizes), jnp.arange(rows * top), side="right").astype(jnp.int32)
    grid = labels.reshape(top, rows).T
    grid = grid[jax.random.permutation(jax.random.fold_in(own, 1), rows)]
    turn = jax.random.randint(jax.random.fold_in(own, 2), (rows, 1), 0, top)
    return jnp.take_along_axis(grid, (jnp.arange(top)[None, :] + turn) % top, axis=1)


def load_shares(number_of, total, most, lean, full):
    portions = [(1 << 20) // math.isqrt(standing ** lean) + 1 for standing in range(1, number_of + 1)]
    largest = most if full else min(most, max(-(-total // number_of), total * portions[0] // sum(portions)))
    least = 1 if total - largest >= number_of - 1 else 0
    holding, surplus = [largest] + [least] * (number_of - 1), total - largest - least * (number_of - 1)
    while surplus > 0:
        candidates = [i for i in range(1, number_of) if holding[i] < largest] or [i for i in range(1, number_of) if holding[i] < most]
        pool, left = sum([portions[i] for i in candidates]), surplus
        for i in candidates:
            more = min(most - holding[i], max(1, left * portions[i] // pool), surplus)
            holding[i] = holding[i] + more
            surplus = surplus - more
    return np.array(holding)


def bell_draw(key, dims, width, limit, cuts=(), kind=jnp.bfloat16):
    values = jax.random.normal(key, dims, jnp.float32) * width
    if len(cuts) > 0:
        values = shard_levels(key, dims, cuts, -0.22, 0.18) * values
    return jnp.clip(values, min=-limit, max=limit).astype(kind)


def setup_inputs(seed: int = 0) -> dict:
    streams_of = jax.random.split(jax.random.key(seed), 8)
    valence = bell_draw(streams_of[0], (PAIRS, VP, NG), 1.0, 6.0, ((0, 64), (1, 4)), jnp.float32)
    conduction = bell_draw(streams_of[1], (PAIRS, CP, NG), (NG * VC * 2 * PAIR_DEV) ** -0.5, 0.0024414062, ((0, 64), (2, 4)))
    screened = draw_screened(jax.random.fold_in(streams_of[7], 71), 0)
    momentum_keys = jax.random.split(jax.random.fold_in(streams_of[3], 1), PAIRS // PAIR_DEV)
    momentum_turns = jax.random.permutation(jax.random.fold_in(streams_of[3], 3), PAIRS // PAIR_DEV)
    momentum = jax.vmap(lambda own, number: routed_block(jax.random.fold_in(streams_of[3], 2), own, number, PAIR_DEV, Q, 1, CAP, 2))(momentum_keys, momentum_turns).reshape((PAIRS, 1))
    kpairs = touch_ends(jax.random.randint(streams_of[4], (PAIRS, 2), 0, NK), jax.random.fold_in(streams_of[4], 1), 0, NK - 1).astype(jnp.int32)
    kpoint_slot = jax.random.permutation(streams_of[5], NK).astype(jnp.int32)
    trial_blocks = bell_draw(streams_of[6], (NK, NTRIAL * VC), 1.0, 6.0, ((0, 64), (1, 4)), jnp.float32)
    return dict(valence=valence, conduction=conduction, screened=screened, momentum=momentum, kpairs=kpairs, kpoint_slot=kpoint_slot, trial_blocks=trial_blocks)


def reference(valence, conduction, screened, momentum, kpairs, kpoint_slot, trial_blocks):
    highest = lax.Precision.HIGHEST

    def screen_pair(items):
        rows_in, conduct, index = items
        matrix = lax.dynamic_index_in_dim(screened, index, 0, keepdims=False)
        screened_rows = jnp.dot(rows_in, matrix, precision=highest, preferred_element_type=jnp.float32)
        conduct_wide = conduct.astype(jnp.float32)
        return jnp.dot(screened_rows, conduct_wide.T, precision=highest, preferred_element_type=jnp.float32)

    kernel = lax.map(screen_pair, (valence, conduction, momentum[:, 0].astype(jnp.int32)))
    kernel_blocks = kernel.reshape(PAIRS, VB, VB, CB, CB)
    slot_near = jnp.take(kpoint_slot, kpairs[:, 0].astype(jnp.int32)).astype(jnp.int32)
    slot_far = jnp.take(kpoint_slot, kpairs[:, 1].astype(jnp.int32)).astype(jnp.int32)
    blocks = trial_blocks.reshape(NK, NTRIAL, VB, CB)
    near_trials = jnp.take(blocks, slot_near, axis=0)
    far_trials = jnp.take(blocks, slot_far, axis=0)
    direct = jnp.einsum("pvwcd,pnwd->pnvc", kernel_blocks, far_trials, precision=highest)
    mirror = jnp.einsum("pvwcd,pnvc->pnwd", kernel_blocks, near_trials, precision=highest)
    result = jnp.zeros((NK, NTRIAL, VB, CB), jnp.float32)
    result = result.at[slot_near].add(direct)
    result = result.at[slot_far].add(mirror)
    return result.reshape(NK, NTRIAL * VB * CB)
```

```python
import functools
import jax
import jax.numpy as jnp
from jax import lax
from jax.experimental import pallas as pl
from jax.experimental.pallas import tpu as pltpu
from jax.sharding import PartitionSpec as P

VB = 8
CB = 14
CD = 16
VC = VB * CD
F32 = jnp.float32
BF16 = jnp.bfloat16


def split(x):
    high = x.astype(BF16)
    return high, (x - high.astype(F32)).astype(BF16)


def mul(a, b, dims):
    return lax.dot_general(a, b, (dims, ((), ())), preferred_element_type=F32)


def mul3(a, b, dims=((1,), (0,))):
    rows = a.shape[0]
    a_high, a_low = split(a)
    b_high, b_low = split(b)
    both = mul(jnp.concatenate([a_high, a_low], axis=0), b_high, dims)
    return both[:rows] + both[rows:] + mul(a_high, b_low, dims)


def kernel_body(momentum_ref, valence_ref, matrix_ref, conduct_ref, out_ref, low_ref, high_ref, turn_ref):
    rows = valence_ref.shape[0] * valence_ref.shape[2]
    valence = valence_ref[...].reshape(rows, valence_ref.shape[3])
    screened_rows = mul3(valence, matrix_ref[0])
    rows_high, rows_low = split(screened_rows)
    both = mul(jnp.concatenate([rows_high, rows_low], axis=0), conduct_ref[0], ((1,), (1,)))
    kernel = both[:rows] + both[rows:]
    low_ref[...] = kernel[:, :VC]
    high_ref[...] = jnp.concatenate([kernel[:, VC:], jnp.zeros((rows, 2 * VC - kernel.shape[1]), F32)], axis=1)
    group = lax.broadcasted_iota(jnp.int32, (VB, VC), 1) // CD
    for half, ref in enumerate((low_ref, high_ref)):
        tiles = [ref[pl.ds(w, VB, stride=VB), :] for w in range(VB)]
        for step in (4, 2, 1):
            upper = (group & step) != 0
            for i in range(VB):
                if i & step:
                    continue
                a, b = tiles[i], tiles[i + step]
                tiles[i] = jnp.where(upper, pltpu.roll(b, step * CD, axis=1), a)
                tiles[i + step] = jnp.where(upper, b, pltpu.roll(a, VC - step * CD, axis=1))
        for i in range(VB):
            turn_ref[pl.ds((half * VB + i) * VB, VB), :] = tiles[i]
    for v in range(VB):
        out_ref[0, pl.ds(v * CD, CD), :] = turn_ref[pl.ds(v, CD, stride=VB), :]


def pair_kernels(momentum, valence, matrices, conduction):
    parts, pairs, rows, waves = valence.shape
    own = matrices.shape[2]
    columns = conduction.shape[1]
    return pl.pallas_call(
        kernel_body,
        out_shape=jax.ShapeDtypeStruct((pairs, VC, VC), F32),
        grid_spec=pltpu.PrefetchScalarGridSpec(
            num_scalar_prefetch=1,
            grid=(pairs,),
            in_specs=[
                pl.BlockSpec((parts, 1, rows, waves), lambda p, q: (0, p, 0, 0)),
                pl.BlockSpec((1, waves, own), lambda p, q: (q[p], 0, 0)),
                pl.BlockSpec((1, columns, own), lambda p, q: (p, 0, 0)),
            ],
            out_specs=pl.BlockSpec((1, VC, VC), lambda p, q: (p, 0, 0)),
            scratch_shapes=[
                pltpu.VMEM((VB * VB, VC), F32),
                pltpu.VMEM((VB * VB, VC), F32),
                pltpu.VMEM((VC, VC), F32),
            ],
        ),
        cost_estimate=pl.CostEstimate(flops=6 * pairs * 64 * waves * own, bytes_accessed=pairs * waves * own * 4, transcendentals=0),
    )(momentum, valence, matrices, conduction)


def response_body(near_ref, far_ref, kernel_ref, trial_ref, out_ref):
    out_ref[...] = jnp.zeros_like(out_ref)

    @pl.loop(0, kernel_ref.shape[0])
    def _(p):
        near, far = near_ref[p], far_ref[p]
        kernel = kernel_ref[p]
        direct = mul3(trial_ref[far], kernel, ((1,), (1,)))
        mirror = mul3(trial_ref[near], kernel, ((1,), (0,)))
        out_ref[near] = out_ref[near] + direct
        out_ref[far] = out_ref[far] + mirror


def contributions(near, far, kernel, trials):
    whole = pl.BlockSpec(memory_space=pltpu.VMEM)
    scalar = pl.BlockSpec(memory_space=pltpu.SMEM)
    return pl.pallas_call(
        response_body,
        out_shape=jax.ShapeDtypeStruct(trials.shape, F32),
        in_specs=[scalar, scalar, whole, whole],
        out_specs=whole,
        cost_estimate=pl.CostEstimate(flops=12 * kernel.size * trials.shape[1], bytes_accessed=4 * (kernel.size + 2 * trials.size), transcendentals=0),
    )(near, far, kernel, trials)


def sum_over_ka(x, ka):
    swap = [(i, i ^ 1) for i in range(ka)]
    fold = [(i, ka - 1 - i) for i in range(ka)]
    half = x.shape[0] // 2
    a, b = x[:half], x[half:]
    a_in, b_in = lax.ppermute(a, "ka", swap), lax.ppermute(b, "ka", fold)
    a, b = a + a_in, b + b_in
    a_in, b_in = lax.ppermute(a, "ka", fold), lax.ppermute(b, "ka", swap)
    return jnp.concatenate([a + a_in, b + b_in], axis=0)


def local(valence, conduction, screened, momentum, kpairs, kpoint_slot, trial_blocks):
    owners, ka = lax.axis_size("pb"), lax.axis_size("ka")
    pair_dev = valence.shape[0]
    own = conduction.shape[2]
    column = lax.axis_index("ka") * own
    piece = lax.dynamic_slice(screened[0], (0, column), (screened.shape[1], own))
    matrices = lax.all_gather(piece, "pb")
    spread = jnp.broadcast_to(valence[None], (ka,) + valence.shape)
    rows = lax.all_to_all(spread, "ka", split_axis=0, concat_axis=0, tiled=True)
    own_trials = trial_blocks.reshape(-1, VB, CB)
    local_trials = own_trials.shape[0]
    own_trials = jnp.pad(own_trials, ((0, 0), (0, 0), (0, CD - CB))).reshape(1, local_trials, VC)
    spread = jnp.broadcast_to(own_trials, (owners, local_trials, VC))
    trials = lax.all_to_all(spread, "pb", split_axis=0, concat_axis=0, tiled=True)
    conduct = conduction.reshape(pair_dev, CB, CB, own)
    conduct = jnp.pad(conduct, ((0, 0), (0, 0), (0, CD - CB), (0, 0))).reshape(pair_dev, CB * CD, own)
    near = jnp.take(kpoint_slot, kpairs[:, 0])
    far = jnp.take(kpoint_slot, kpairs[:, 1])
    rows, conduct, trials, near, far = lax.optimization_barrier((rows, conduct, trials, near, far))
    kernel = sum_over_ka(pair_kernels(momentum[:, 0], rows, matrices, conduct), ka)
    summed = contributions(near, far, kernel, trials)
    parts = lax.all_to_all(summed, "pb", split_axis=0, concat_axis=0, tiled=True)
    response = jnp.sum(parts, axis=0).reshape(local_trials, VB, CD)[:, :, :CB]
    return response.reshape(1, -1)


def solution(mesh):
    return jax.shard_map(
        local,
        mesh=mesh,
        in_specs=(
            P("pb", "ka", None),
            P("pb", None, "ka"),
            P("pb", None, None),
            P("pb", None),
            P("pb", None),
            P(),
            P("pb", "ka"),
        ),
        out_specs=P("pb", "ka"),
        check_vma=False,
    )
```

```python
import jax
import jax.numpy as jnp
from jax import lax
from jax.experimental import pallas as pl
from jax.experimental.pallas import tpu as pltpu
from jax.sharding import PartitionSpec as P

VB = 8
CB = 14
CD = 16
VC = VB * CD
F32 = jnp.float32
BF16 = jnp.bfloat16
PLAIN = ((1,), (0,))
TURNED = ((1,), (1,))


def split(x):
    high = x.astype(BF16)
    return high, (x - high.astype(F32)).astype(BF16)


def mul(a, b, dims):
    return lax.dot_general(a, b, (dims, ((), ())), preferred_element_type=F32)


def mul3(a, b, dims=PLAIN):
    rows = a.shape[0]
    a_high, a_low = split(a)
    b_high, b_low = split(b)
    both = mul(jnp.concatenate([a_high, a_low], axis=0), b_high, dims)
    return both[:rows] + both[rows:] + mul(a_high, b_low, dims)


def flat(ref):
    return ref[...].reshape(ref.shape[0] * ref.shape[2], ref.shape[3])


def opposite_body(momentum_ref, ka_ref, own_ref, other_ref, quads_ref, keep_ref, send_ref):
    half = own_ref.shape[3] // 2
    own, other = flat(own_ref), flat(other_ref)
    first = ka_ref[0] < 2
    quad_a, quad_b = quads_ref[0, :half, :], quads_ref[0, half:, :]
    other_a = jnp.where(first, other[:, :half], other[:, half:])
    other_b = jnp.where(first, other[:, half:], other[:, :half])
    keep_ref[0] = jnp.concatenate([mul3(other_a, quad_a, TURNED), mul3(other_b, quad_b, TURNED)], axis=1)
    send_a, send_b = mul3(own[:, :half], quad_a), mul3(own[:, half:], quad_b)
    send_ref[0, :, :half] = jnp.where(first, send_a, send_b)
    send_ref[0, :, half:] = jnp.where(first, send_b, send_a)


def next_body(momentum_ref, ka_ref, own_ref, other_ref, block_ref, keep_ref, send_ref):
    block = block_ref[0]
    keep_ref[0] = mul3(flat(other_ref), block, TURNED)
    send_ref[0] = mul3(flat(own_ref), block)


def off_diagonal(body, distance, momentum, ka, valence, blocks):
    parts, pairs, rows, waves = valence.shape
    own = waves // parts
    shape = jax.ShapeDtypeStruct((pairs, parts * rows, own), F32)
    result = pl.BlockSpec((1, parts * rows, own), lambda p, q, y: (p, 0, 0))
    return pl.pallas_call(
        body,
        out_shape=(shape, shape),
        grid_spec=pltpu.PrefetchScalarGridSpec(
            num_scalar_prefetch=2,
            grid=(pairs,),
            in_specs=[
                pl.BlockSpec((parts, 1, rows, own), lambda p, q, y: (0, p, 0, y[0])),
                pl.BlockSpec((parts, 1, rows, own), lambda p, q, y: (0, p, 0, (y[0] + distance) % parts)),
                pl.BlockSpec((1,) + blocks.shape[1:], lambda p, q, y: (q[p], 0, 0)),
            ],
            out_specs=(result, result),
        ),
        cost_estimate=pl.CostEstimate(
            flops=12 * pairs * parts * rows * blocks.shape[1] * blocks.shape[2],
            bytes_accessed=pairs * blocks.shape[1] * blocks.shape[2] * 4,
            transcendentals=0,
        ),
    )(momentum, ka, valence, valence, blocks)


def diagonal_body(momentum_ref, ka_ref, own_ref, quads_ref, add1_ref, add2_ref, add3_ref, add4_ref, conduct_ref, out_ref, low_ref, high_ref):
    half = own_ref.shape[3] // 2
    own = flat(own_ref)
    rows = own.shape[0]
    own_a, own_b = own[:, :half], own[:, half:]
    quads = quads_ref[0]
    turned = mul3(own_b, quads[:, half : 2 * half], TURNED)
    product = mul3(own_a, quads[:, : 2 * half]) + jnp.concatenate([turned, mul3(own_b, quads[:, 2 * half :])], axis=1)
    product = product + ((add1_ref[0] + add2_ref[0]) + (add3_ref[0] + add4_ref[0]))
    high, low = split(product)
    both = mul(jnp.concatenate([high, low], axis=0), conduct_ref[0], TURNED)
    kernel = both[:rows] + both[rows:]
    low_ref[...] = kernel[:, :VC]
    high_ref[...] = jnp.concatenate([kernel[:, VC:], jnp.zeros((rows, 2 * VC - kernel.shape[1]), F32)], axis=1)
    group = lax.broadcasted_iota(jnp.int32, (VB, VC), 1) // CD
    for number, ref in enumerate((low_ref, high_ref)):
        tiles = [ref[pl.ds(w, VB, stride=VB), :] for w in range(VB)]
        for step in (4, 2, 1):
            upper = (group & step) != 0
            for i in range(VB):
                if i & step:
                    continue
                a, b = tiles[i], tiles[i + step]
                tiles[i] = jnp.where(upper, pltpu.roll(b, step * CD, axis=1), a)
                tiles[i + step] = jnp.where(upper, b, pltpu.roll(a, VC - step * CD, axis=1))
        for i in range(VB):
            c = number * VB + i
            if c < CB:
                out_ref[0, c * VB : (c + 1) * VB, :] = tiles[i]


def diagonal(start, count, momentum, ka, valence, quads, adds, conduction):
    parts, pairs, rows, waves = valence.shape
    own = waves // parts
    columns = conduction.shape[1]
    add = pl.BlockSpec((1, parts * rows, own), lambda p, q, y: (start + p, 0, 0))
    return pl.pallas_call(
        diagonal_body,
        out_shape=jax.ShapeDtypeStruct((count, VB * CB, VC), F32),
        grid_spec=pltpu.PrefetchScalarGridSpec(
            num_scalar_prefetch=2,
            grid=(count,),
            in_specs=[
                pl.BlockSpec((parts, 1, rows, own), lambda p, q, y: (0, start + p, 0, y[0])),
                pl.BlockSpec((1,) + quads.shape[1:], lambda p, q, y: (q[start + p], 0, 0)),
                add,
                add,
                add,
                add,
                pl.BlockSpec((1, columns, own), lambda p, q, y: (start + p, 0, 0)),
            ],
            out_specs=pl.BlockSpec((1, VB * CB, VC), lambda p, q, y: (p, 0, 0)),
            scratch_shapes=[pltpu.VMEM((VB * VB, VC), F32), pltpu.VMEM((VB * VB, VC), F32)],
        ),
        cost_estimate=pl.CostEstimate(flops=6 * count * 64 * own * own, bytes_accessed=count * own * own * 12, transcendentals=0),
    )(momentum, ka, valence, quads, *adds, conduction)


def response_body(near_ref, far_ref, first_ref, second_ref, trial_ref, out_ref, turn_ref):
    out_ref[...] = jnp.zeros_like(out_ref)
    turn_ref[...] = jnp.zeros_like(turn_ref)
    for start, kernel_ref in ((0, first_ref), (first_ref.shape[0], second_ref)):

        @pl.loop(0, kernel_ref.shape[0])
        def _(p, start=start, kernel_ref=kernel_ref):
            near, far = near_ref[start + p], far_ref[start + p]
            for v in range(VB):
                turn_ref[v * CD : v * CD + CB, :] = kernel_ref[p, pl.ds(v, CB, stride=VB), :]
            kernel = turn_ref[...]
            direct = mul3(trial_ref[far], kernel, TURNED)
            mirror = mul3(trial_ref[near], kernel, PLAIN)
            out_ref[near] = out_ref[near] + direct
            out_ref[far] = out_ref[far] + mirror


def contributions(near, far, first, second, trials):
    whole = pl.BlockSpec(memory_space=pltpu.VMEM)
    scalar = pl.BlockSpec(memory_space=pltpu.SMEM)
    size = first.size + second.size
    return pl.pallas_call(
        response_body,
        out_shape=jax.ShapeDtypeStruct(trials.shape, F32),
        in_specs=[scalar, scalar, whole, whole, whole],
        out_specs=whole,
        scratch_shapes=[pltpu.VMEM((VC, VC), F32)],
        cost_estimate=pl.CostEstimate(flops=12 * size * trials.shape[1], bytes_accessed=4 * (size + 2 * trials.size), transcendentals=0),
    )(near, far, first, second, trials)


def local(valence, conduction, screened, momentum, kpairs, kpoint_slot, trial_blocks):
    ka = lax.axis_size("ka")
    pair_dev = valence.shape[0]
    own = conduction.shape[2]
    half = own // 2
    here = lax.axis_index("ka").astype(jnp.int32)
    target = momentum[:, 0]
    matrix = screened[0]

    def block(row, column, rows, columns):
        return lax.dynamic_slice(matrix, (row, column), (rows, columns))

    top = here * own
    across = lax.rem(here + 2, ka) * own
    side = jnp.where(here < 2, 0, half)
    opposite = jnp.concatenate([block(top, across + side, half, half), block(top + half, across + half - side, half, half)], axis=0)
    beside = block(top, lax.rem(here + 1, ka) * own, own, own)
    middle = jnp.concatenate([block(top, top, half, own), block(top + half, top + half, half, half)], axis=1)
    opposite = lax.all_gather(opposite, "pb")
    beside = lax.all_gather(beside, "pb")
    middle = lax.all_gather(middle, "pb")

    spread = jnp.broadcast_to(valence[None], (ka,) + valence.shape)
    rows = lax.all_to_all(spread, "ka", split_axis=0, concat_axis=0, tiled=True)
    own_trials = trial_blocks.reshape(-1, VB, CB)
    local_trials = own_trials.shape[0]
    own_trials = jnp.pad(own_trials, ((0, 0), (0, 0), (0, CD - CB))).reshape(local_trials, VC)
    trials = lax.all_gather(own_trials, "pb")
    conduct = conduction.reshape(pair_dev, CB, CB, own)
    conduct = jnp.pad(conduct, ((0, 0), (0, 0), (0, CD - CB), (0, 0))).reshape(pair_dev, CB * CD, own)
    near = jnp.take(kpoint_slot, kpairs[:, 0])
    far = jnp.take(kpoint_slot, kpairs[:, 1])
    rows, conduct, near, far = lax.optimization_barrier((rows, conduct, near, far))

    here = here.reshape(1)
    keep2, send2 = off_diagonal(opposite_body, 2, target, here, rows, opposite)
    came2 = lax.ppermute(send2, "ka", [(i, (i + 2) % ka) for i in range(ka)])
    keep1, send1 = off_diagonal(next_body, 1, target, here, rows, beside)
    came1 = lax.ppermute(send1, "ka", [(i, (i + 1) % ka) for i in range(ka)])

    swap = [(i, i ^ 1) for i in range(ka)]
    fold = [(i, ka - 1 - i) for i in range(ka)]
    adds = (keep1, keep2, came1, came2)
    cut = pair_dev // 2
    first = diagonal(0, cut, target, here, rows, middle, adds, conduct)
    second = diagonal(cut, pair_dev - cut, target, here, rows, middle, adds, conduct)
    first = first + lax.ppermute(first, "ka", swap)
    second = second + lax.ppermute(second, "ka", fold)
    first = first + lax.ppermute(first, "ka", fold)
    second = second + lax.ppermute(second, "ka", swap)

    summed = contributions(near, far, first, second, trials)
    parts = lax.all_to_all(summed, "pb", split_axis=0, concat_axis=0, tiled=True)
    response = jnp.sum(parts, axis=0).reshape(local_trials, VB, CD)[:, :, :CB]
    return response.reshape(1, -1)


def solution(mesh):
    return jax.shard_map(
        local,
        mesh=mesh,
        in_specs=(
            P("pb", "ka", None),
            P("pb", None, "ka"),
            P("pb", None, None),
            P("pb", None),
            P("pb", None),
            P(),
            P("pb", "ka"),
        ),
        out_specs=P("pb", "ka"),
        check_vma=False,
    )
```

```python
import jax
import jax.numpy as jnp
from jax import lax
from jax.experimental import pallas as pl
from jax.experimental.pallas import tpu as pltpu
from jax.sharding import PartitionSpec as P

VB = 8
CB = 14
CD = 16
VC = VB * CD
F32 = jnp.float32
BF16 = jnp.bfloat16
PLAIN = ((1,), (0,))
TURNED = ((1,), (1,))


def split(x):
    high = x.astype(BF16)
    return high, (x - high.astype(F32)).astype(BF16)


def mul(a, b, dims):
    return lax.dot_general(a, b, (dims, ((), ())), preferred_element_type=F32)


def mul3(a, b, dims=PLAIN):
    rows = a.shape[0]
    a_high, a_low = split(a)
    b_high, b_low = split(b)
    both = mul(jnp.concatenate([a_high, a_low], axis=0), b_high, dims)
    return both[:rows] + both[rows:] + mul(a_high, b_low, dims)


def pair_body(momentum_ref, ka_ref, *refs):
    parts = len(refs) // 3 - 2
    valence_refs = refs[: 3 * parts]
    blocks_ref, conduct_ref, conduct_next_ref, out_ref, low_ref, high_ref = refs[3 * parts :]
    own, beside, across = (
        jnp.concatenate([ref[0] for ref in valence_refs[i * parts : (i + 1) * parts]], axis=0) for i in range(3)
    )
    rows, width = own.shape
    half = width // 2
    blocks = blocks_ref[0]
    corner = blocks[:, half : 2 * half]
    start = 3 * half
    next_block = jnp.concatenate([blocks[:, start : start + width], blocks[:, start + width : start + 2 * width]], axis=0)
    start += 2 * width
    far_block = jnp.concatenate([blocks[:, start : start + width], blocks[:, start + width : start + 2 * width]], axis=0)
    below = jnp.concatenate([mul3(own[:, half:], corner, TURNED), mul3(own[:, half:], blocks[:, 2 * half : 3 * half])], axis=1)
    here = mul3(own[:, :half], blocks[:, : 2 * half]) + below + mul3(beside, next_block) + mul3(across, far_block)
    there = mul3(own, next_block, TURNED)
    product = jnp.concatenate([here, there], axis=1)
    high, low = split(product)
    conduct = jnp.concatenate([conduct_ref[0], conduct_next_ref[0].astype(BF16)], axis=1)
    both = mul(jnp.concatenate([high, low], axis=0), conduct, TURNED)
    kernel = both[:rows] + both[rows:]
    each = rows // parts
    rest = jnp.zeros((each, 2 * VC - kernel.shape[1]), F32)
    for k in range(parts):
        place = pl.ds(pl.multiple_of(lax.rem(ka_ref[0] + parts - k, parts) * each, each), each)
        part = kernel[k * each : (k + 1) * each]
        low_ref[place, :] = part[:, :VC]
        high_ref[place, :] = jnp.concatenate([part[:, VC:], rest], axis=1)
    group = lax.broadcasted_iota(jnp.int32, (VB, VC), 1) // CD
    for number, ref in enumerate((low_ref, high_ref)):
        tiles = [ref[pl.ds(w, VB, stride=VB), :] for w in range(VB)]
        for step in (4, 2, 1):
            upper = (group & step) != 0
            for i in range(VB):
                if i & step:
                    continue
                a, b = tiles[i], tiles[i + step]
                tiles[i] = jnp.where(upper, pltpu.roll(b, step * CD, axis=1), a)
                tiles[i + step] = jnp.where(upper, b, pltpu.roll(a, VC - step * CD, axis=1))
        for i in range(VB):
            c = number * VB + i
            if c < CB:
                out_ref[0, c * VB : (c + 1) * VB, :] = tiles[i]


def pair_kernels(start, count, momentum, ka, valence, blocks, conduction, conduction_next):
    pairs, rows, waves = valence[0].shape
    parts = len(valence)
    own = waves // parts
    columns = conduction.shape[1]

    def column(i):
        return pl.BlockSpec((1, rows, own), lambda p, q, y: (start + p, 0, (y[0] + i) % parts))

    conduct = pl.BlockSpec((1, columns, own), lambda p, q, y: (start + p, 0, 0))
    return pl.pallas_call(
        pair_body,
        out_shape=jax.ShapeDtypeStruct((count, VB * CB, VC), F32),
        grid_spec=pltpu.PrefetchScalarGridSpec(
            num_scalar_prefetch=2,
            grid=(count,),
            in_specs=[column(i) for i in range(3) for _ in range(parts)]
            + [pl.BlockSpec((1,) + blocks.shape[1:], lambda p, q, y: (q[start + p], 0, 0)), conduct, conduct],
            out_specs=pl.BlockSpec((1, VB * CB, VC), lambda p, q, y: (p, 0, 0)),
            scratch_shapes=[pltpu.VMEM((VB * VB, VC), F32), pltpu.VMEM((VB * VB, VC), F32)],
        ),
        cost_estimate=pl.CostEstimate(flops=24 * count * 64 * own * own, bytes_accessed=count * own * own * 12, transcendentals=0),
    )(momentum, ka, *(valence * 3), blocks, conduction, conduction_next)


def response_body(near_ref, far_ref, first_ref, second_ref, trial_ref, out_ref, turn_ref):
    out_ref[...] = jnp.zeros_like(out_ref)
    turn_ref[...] = jnp.zeros_like(turn_ref)
    for start, kernel_ref in ((0, first_ref), (first_ref.shape[0], second_ref)):

        @pl.loop(0, kernel_ref.shape[0])
        def _(p, start=start, kernel_ref=kernel_ref):
            near, far = near_ref[start + p], far_ref[start + p]
            for v in range(VB):
                turn_ref[v * CD : v * CD + CB, :] = kernel_ref[p, pl.ds(v, CB, stride=VB), :]
            kernel = turn_ref[...]
            direct = mul3(trial_ref[far], kernel, TURNED)
            mirror = mul3(trial_ref[near], kernel, PLAIN)
            out_ref[near] = out_ref[near] + direct
            out_ref[far] = out_ref[far] + mirror


def contributions(near, far, first, second, trials):
    whole = pl.BlockSpec(memory_space=pltpu.VMEM)
    scalar = pl.BlockSpec(memory_space=pltpu.SMEM)
    size = first.size + second.size
    return pl.pallas_call(
        response_body,
        out_shape=jax.ShapeDtypeStruct(trials.shape, F32),
        in_specs=[scalar, scalar, whole, whole, whole],
        out_specs=whole,
        scratch_shapes=[pltpu.VMEM((VC, VC), F32)],
        cost_estimate=pl.CostEstimate(flops=12 * size * trials.shape[1], bytes_accessed=4 * (size + 2 * trials.size), transcendentals=0),
    )(near, far, first, second, trials)


def local(valence, conduction, screened, momentum, kpairs, kpoint_slot, trial_blocks):
    ka = lax.axis_size("ka")
    pair_dev = valence.shape[0]
    own = conduction.shape[2]
    half = own // 2
    here = lax.axis_index("ka").astype(jnp.int32)
    target = momentum[:, 0]
    matrix = screened[0]

    def block(row, column, rows, columns):
        return lax.dynamic_slice(matrix, (row, column), (rows, columns))

    top = here * own
    beside, across = lax.rem(here + 1, ka) * own, lax.rem(here + 2, ka) * own
    pieces = [block(top, top, half, own), block(top + half, top + half, half, half)]
    pieces += [block(row + side, top, half, own) for row in (beside, across) for side in (0, half)]
    blocks = lax.all_gather(jnp.concatenate(pieces, axis=1), "pb")

    own_trials = trial_blocks.reshape(-1, VB, CB)
    local_trials = own_trials.shape[0]
    own_trials = jnp.pad(own_trials, ((0, 0), (0, 0), (0, CD - CB))).reshape(local_trials, VC)
    trials = lax.all_gather(own_trials, "pb")
    ahead = [(i, (i + 1) % ka) for i in range(ka)]
    back = [((i + 1) % ka, i) for i in range(ka)]
    conduct = conduction.reshape(pair_dev, CB, CB, own)
    conduct = jnp.pad(conduct, ((0, 0), (0, 0), (0, CD - CB), (0, 0))).reshape(pair_dev, CB * CD, own)
    conduct_next = lax.ppermute(conduct.astype(F32), "ka", back)
    rows = [valence]
    for _ in range(ka - 1):
        rows.append(lax.ppermute(rows[-1], "ka", ahead))
    near = jnp.take(kpoint_slot, kpairs[:, 0])
    far = jnp.take(kpoint_slot, kpairs[:, 1])
    rows, conduct, conduct_next, near, far = lax.optimization_barrier((rows, conduct, conduct_next, near, far))

    here = here.reshape(1)
    swap = [(i, i ^ 1) for i in range(ka)]
    fold = [(i, ka - 1 - i) for i in range(ka)]
    cut = pair_dev // 2
    first = pair_kernels(0, cut, target, here, rows, blocks, conduct, conduct_next)
    second = pair_kernels(cut, pair_dev - cut, target, here, rows, blocks, conduct, conduct_next)
    first = first + lax.ppermute(first, "ka", swap)
    second = second + lax.ppermute(second, "ka", fold)
    first = first + lax.ppermute(first, "ka", fold)
    second = second + lax.ppermute(second, "ka", swap)

    summed = contributions(near, far, first, second, trials)
    parts = lax.all_to_all(summed, "pb", split_axis=0, concat_axis=0, tiled=True)
    response = jnp.sum(parts, axis=0).reshape(local_trials, VB, CD)[:, :, :CB]
    return response.reshape(1, -1)


def solution(mesh):
    return jax.shard_map(
        local,
        mesh=mesh,
        in_specs=(
            P("pb", "ka", None),
            P("pb", None, "ka"),
            P("pb", None, None),
            P("pb", None),
            P("pb", None),
            P(),
            P("pb", "ka"),
        ),
        out_specs=P("pb", "ka"),
        check_vma=False,
    )
```

```python
import jax
import jax.numpy as jnp
import numpy as np
from jax import lax
from jax.experimental import pallas as pl
from jax.experimental.pallas import tpu as pltpu
from jax.sharding import PartitionSpec as P

VB = 8
CB = 14
CD = 16
VC = VB * CD
PAIR = 2
F32 = jnp.float32
BF16 = jnp.bfloat16
PLAIN = ((1,), (0,))
TURNED = ((1,), (1,))


def split(x):
    high = x.astype(BF16)
    return high, (x - high.astype(F32)).astype(BF16)


def mul(a, b, dims):
    return lax.dot_general(a, b, (dims, ((), ())), preferred_element_type=F32)


def mul3(a, b, dims=PLAIN):
    rows = a.shape[0]
    a_high, a_low = split(a)
    b_high, b_low = split(b)
    both = mul(jnp.concatenate([a_high, a_low], axis=0), b_high, dims)
    return both[:rows] + both[rows:] + mul(a_high, b_low, dims)


def quads(x, half):
    return [x[i : i + half, j : j + half] for i in (0, half) for j in (0, half)]


def pack_body(ka_ref, trial_ref, spread_ref, own_ref, beside_ref, across_ref, out_ref):
    trials = trial_ref.shape[0]
    half = own_ref.shape[1] // 2
    out_ref[:trials, :] = jnp.dot(trial_ref[...], spread_ref[...], precision=lax.Precision.HIGHEST, preferred_element_type=F32)
    row = lax.broadcasted_iota(jnp.int32, (half, half), 0)
    column = lax.broadcasted_iota(jnp.int32, (half, half), 1)
    a, b, _, d = quads(own_ref[0], half)
    squares = [jnp.where(row <= column, a, d), b] + quads(beside_ref[0], half) + quads(across_ref[0], half)
    for i, square in enumerate(squares):
        start = trials + i * half
        out_ref[start : start + half, :] = square
    line = jnp.sum(jnp.where(row == column, d, 0.0), axis=0, keepdims=True)
    start = trials + len(squares) * half
    out_ref[start:, :] = jnp.broadcast_to(line, (out_ref.shape[0] - start, half))


def pack(ka, trials, spread, screened, parts):
    own = screened.shape[1] // parts
    half = own // 2

    def block(i):
        return pl.BlockSpec((1, own, own), lambda g, y: (0, (y[0] + i) % parts, y[0]))

    rows = trials.shape[0] + 10 * half + 8
    return pl.pallas_call(
        pack_body,
        out_shape=jax.ShapeDtypeStruct((rows, half), F32),
        grid_spec=pltpu.PrefetchScalarGridSpec(
            num_scalar_prefetch=1,
            grid=(1,),
            in_specs=[
                pl.BlockSpec(trials.shape, lambda g, y: (0, 0)),
                pl.BlockSpec(spread.shape, lambda g, y: (0, 0)),
                block(0),
                block(1),
                block(2),
            ],
            out_specs=pl.BlockSpec((rows, half), lambda g, y: (0, 0)),
        ),
    )(ka, trials, spread, screened, screened, screened)


def prepare_body(ka_ref, *refs):
    parts = len(refs) // 3 - 1
    conduct_ref, conduct_next_ref, rows_ref, joined_ref = refs[3 * parts :]
    each, width = refs[0].shape[1:]
    for i in range(3):
        for k in range(parts):
            place = pl.multiple_of(lax.rem(ka_ref[0] + parts - k, parts) * each, each)
            high, low = split(refs[i * parts + k][0])
            rows_ref[0, pl.ds(place, each), i * width : (i + 1) * width] = high
            rows_ref[0, pl.ds(parts * each + place, each), i * width : (i + 1) * width] = low
    joined_ref[0, :, :width] = conduct_ref[0]
    joined_ref[0, :, width:] = conduct_next_ref[0].astype(BF16)


def prepare(ka, valence, conduction, conduction_next):
    pairs, rows, waves = valence[0].shape
    parts = len(valence)
    own = waves // parts
    columns = conduction.shape[1]

    def column(i):
        return pl.BlockSpec((1, rows, own), lambda p, y: (p, 0, (y[0] + i) % parts))

    conduct = pl.BlockSpec((1, columns, own), lambda p, y: (p, 0, 0))
    shapes = (pairs, 2 * parts * rows, 3 * own), (pairs, columns, 2 * own)
    return pl.pallas_call(
        prepare_body,
        out_shape=tuple(jax.ShapeDtypeStruct(shape, BF16) for shape in shapes),
        grid_spec=pltpu.PrefetchScalarGridSpec(
            num_scalar_prefetch=1,
            grid=(pairs,),
            in_specs=[column(i) for i in range(3) for _ in range(parts)] + [conduct, conduct],
            out_specs=tuple(pl.BlockSpec((1,) + shape[1:], lambda p, y: (p, 0, 0)) for shape in shapes),
        ),
        cost_estimate=pl.CostEstimate(flops=0, bytes_accessed=pairs * rows * waves * 40, transcendentals=0),
    )(ka, *(valence * 3), conduction, conduction_next)


def one_pair(rows, blocks, conduct, out_ref, number, low_ref, high_ref, skip):
    half = blocks.shape[1]
    width = 2 * half
    count = rows.shape[0] // 2
    squares = [blocks[skip + i * half : skip + (i + 1) * half] for i in range(10)]
    line = blocks[skip + 10 * half : skip + 10 * half + 1]
    row = lax.broadcasted_iota(jnp.int32, (half, half), 0)
    column = lax.broadcasted_iota(jnp.int32, (half, half), 1)
    shared, corner = squares[:2]
    turned = shared.T
    a = jnp.where(row <= column, shared, turned)
    d = jnp.where(row > column, shared, jnp.where(row == column, line, turned))
    left = jnp.concatenate([a, corner.T, squares[2], squares[4], squares[6], squares[8]], axis=0)
    right = jnp.concatenate([corner, d, squares[3], squares[5], squares[7], squares[9]], axis=0)
    high, low = split(jnp.concatenate([left, right], axis=1))
    both = mul(rows, high, PLAIN)
    here = both[:count] + both[count:] + mul(rows[:count], low, PLAIN)
    both = mul(rows[:, :width], high[width : 2 * width], TURNED)
    there = both[:count] + both[count:] + mul(rows[:count, :width], low[width : 2 * width], TURNED)
    high, low = split(jnp.concatenate([here, there], axis=1))
    both = mul(jnp.concatenate([high, low], axis=0), conduct, TURNED)
    kernel = both[:count] + both[count:]
    low_ref[...] = kernel[:, :VC]
    high_ref[...] = jnp.concatenate([kernel[:, VC:], jnp.zeros((count, 2 * VC - kernel.shape[1]), F32)], axis=1)
    group = lax.broadcasted_iota(jnp.int32, (VB, VC), 1) // CD
    for part, ref in enumerate((low_ref, high_ref)):
        tiles = [ref[pl.ds(w, VB, stride=VB), :] for w in range(VB)]
        for step in (4, 2, 1):
            upper = (group & step) != 0
            for i in range(VB):
                if i & step:
                    continue
                a, b = tiles[i], tiles[i + step]
                tiles[i] = jnp.where(upper, pltpu.roll(b, step * CD, axis=1), a)
                tiles[i + step] = jnp.where(upper, b, pltpu.roll(a, VC - step * CD, axis=1))
        for i in range(VB):
            c = part * VB + i
            if c < CB:
                out_ref[number, c * VB : (c + 1) * VB, :] = tiles[i]


def pair_body(skip, momentum_ref, rows_ref, *refs):
    blocks, (conduct_ref, out_ref), scratch = refs[:PAIR], refs[PAIR : PAIR + 2], refs[PAIR + 2 :]
    for i in range(PAIR):
        one_pair(rows_ref[i], blocks[i][0], conduct_ref[i], out_ref, i, scratch[2 * i], scratch[2 * i + 1], skip)


def pair_kernels(start, count, momentum, rows, blocks, conduct, skip):
    first = start // PAIR

    def block(i):
        return pl.BlockSpec((1,) + blocks.shape[1:], lambda p, q: (q[start + PAIR * p + i], 0, 0))

    return pl.pallas_call(
        lambda *refs: pair_body(skip, *refs),
        out_shape=jax.ShapeDtypeStruct((count, VB * CB, VC), F32),
        grid_spec=pltpu.PrefetchScalarGridSpec(
            num_scalar_prefetch=1,
            grid=(count // PAIR,),
            in_specs=[pl.BlockSpec((PAIR,) + rows.shape[1:], lambda p, q: (first + p, 0, 0))]
            + [block(i) for i in range(PAIR)]
            + [pl.BlockSpec((PAIR,) + conduct.shape[1:], lambda p, q: (first + p, 0, 0))],
            out_specs=pl.BlockSpec((PAIR, VB * CB, VC), lambda p, q: (p, 0, 0)),
            scratch_shapes=[pltpu.VMEM((VB * VB, VC), F32)] * (2 * PAIR),
        ),
        cost_estimate=pl.CostEstimate(flops=count * 10**8, bytes_accessed=count * 11 * 10**5, transcendentals=0),
    )(momentum, rows, *([blocks] * PAIR), conduct)


def response_body(start, counts, near_ref, far_ref, trial_ref, *refs):
    kernels, (out_ref, turn_ref) = refs[: len(counts)], refs[-2:]
    if len(refs) > len(counts) + 2:
        out_ref[...] = refs[len(counts)][...]
    else:
        out_ref[...] = jnp.zeros_like(out_ref)
    turn_ref[...] = jnp.zeros_like(turn_ref)
    for count, kernel_ref in zip(counts, kernels):

        @pl.loop(0, count)
        def _(p, start=start, kernel_ref=kernel_ref):
            near, far = near_ref[start + p], far_ref[start + p]
            for v in range(VB):
                turn_ref[v * CD : v * CD + CB, :] = kernel_ref[p, pl.ds(v, CB, stride=VB), :]
            kernel = turn_ref[...]
            direct = mul3(trial_ref[far], kernel, TURNED)
            mirror = mul3(trial_ref[near], kernel, PLAIN)
            out_ref[near] = out_ref[near] + direct
            out_ref[far] = out_ref[far] + mirror

        start += count


def contributions(start, near, far, blocks, trials, kernels, before=()):
    counts = [kernel.shape[0] for kernel in kernels]
    shape = (blocks.shape[0], trials, VC)
    whole = [pl.BlockSpec(x.shape, lambda g: (0, 0, 0)) for x in kernels]
    result = pl.BlockSpec(shape, lambda g: (0, 0, 0))
    scalar = pl.BlockSpec(memory_space=pltpu.SMEM)
    return pl.pallas_call(
        lambda *refs: response_body(start, counts, *refs),
        out_shape=jax.ShapeDtypeStruct(shape, F32),
        grid=(1,),
        in_specs=[scalar, scalar, result, *whole] + [result] * len(before),
        out_specs=result,
        scratch_shapes=[pltpu.VMEM((VC, VC), F32)],
        cost_estimate=pl.CostEstimate(flops=sum(counts) * 10**7, bytes_accessed=4 * 10**6, transcendentals=0),
    )(near, far, blocks, *kernels, *before)


def local(valence, conduction, screened, momentum, kpairs, kpoint_slot, trial_blocks):
    ka = lax.axis_size("ka")
    pair_dev = valence.shape[0]
    own = conduction.shape[2]
    here = lax.axis_index("ka").astype(jnp.int32).reshape(1)
    own_trials = trial_blocks.reshape(-1, VB * CB)
    local_trials = own_trials.shape[0]
    entry = np.arange(VB * CB)
    spread = np.zeros((VB * CB, VC), np.float32)
    spread[entry, entry // CB * CD + entry % CB] = 1.0
    blocks = lax.all_gather(pack(here, own_trials, jnp.asarray(spread), screened, ka), "pb")

    ahead = [(i, (i + 1) % ka) for i in range(ka)]
    back = [((i + 1) % ka, i) for i in range(ka)]
    conduct = conduction.reshape(pair_dev, CB, CB, own)
    conduct = jnp.pad(conduct, ((0, 0), (0, 0), (0, CD - CB), (0, 0))).reshape(pair_dev, CB * CD, own)
    conduct_next = lax.ppermute(conduct.astype(F32), "ka", back)
    rows = [valence]
    for _ in range(ka - 1):
        rows.append(lax.ppermute(rows[-1], "ka", ahead))
    near = jnp.take(kpoint_slot, kpairs[:, 0])
    far = jnp.take(kpoint_slot, kpairs[:, 1])
    rows, conduct = prepare(here, rows, conduct, conduct_next)
    rows, conduct, near, far = lax.optimization_barrier((rows, conduct, near, far))

    swap = [(i, i ^ 1) for i in range(ka)]
    fold = [(i, ka - 1 - i) for i in range(ka)]
    target = momentum[:, 0]
    each = max(PAIR, pair_dev // 4 // PAIR * PAIR)
    sizes = [pair_dev - 3 * each, each, each, each]
    kernels, start = [], 0
    for size in sizes:
        kernels.append(pair_kernels(start, size, target, rows, blocks, conduct, local_trials))
        start += size
    turns = (swap, fold)
    kernels = [x + lax.ppermute(x, "ka", turns[i % 2]) for i, x in enumerate(kernels)]
    kernels = [x + lax.ppermute(x, "ka", turns[1 - i % 2]) for i, x in enumerate(kernels)]

    summed = contributions(0, near, far, blocks, local_trials, kernels[:2])
    summed = contributions(sum(sizes[:2]), near, far, blocks, local_trials, kernels[2:], (summed,))
    parts = lax.all_to_all(summed, "pb", split_axis=0, concat_axis=0, tiled=True)
    response = jnp.sum(parts, axis=0).reshape(local_trials, VB, CD)[:, :, :CB]
    return response.reshape(1, -1)


def solution(mesh):
    return jax.shard_map(
        local,
        mesh=mesh,
        in_specs=(
            P("pb", "ka", None),
            P("pb", None, "ka"),
            P("pb", None, None),
            P("pb", None),
            P("pb", None),
            P(),
            P("pb", "ka"),
        ),
        out_specs=P("pb", "ka"),
        check_vma=False,
    )
```

```python
import jax
import jax.numpy as jnp
import numpy as np
from jax import lax
from jax.experimental import pallas as pl
from jax.experimental.pallas import tpu as pltpu
from jax.sharding import PartitionSpec as P

VB = 8
CB = 14
CD = 16
VC = VB * CD
PAIR = 2
F32 = jnp.float32
BF16 = jnp.bfloat16
PLAIN = ((1,), (0,))
TURNED = ((1,), (1,))


def split(x):
    high = x.astype(BF16)
    return high, (x - high.astype(F32)).astype(BF16)


def mul(a, b, dims):
    return lax.dot_general(a, b, (dims, ((), ())), preferred_element_type=F32)


def mul3(a, b, dims=PLAIN):
    rows = a.shape[0]
    a_high, a_low = split(a)
    b_high, b_low = split(b)
    both = mul(jnp.concatenate([a_high, a_low], axis=0), b_high, dims)
    return both[:rows] + both[rows:] + mul(a_high, b_low, dims)


def quads(x, half):
    return [x[i : i + half, j : j + half] for i in (0, half) for j in (0, half)]


def pack_body(ka_ref, trial_ref, spread_ref, own_ref, beside_ref, across_ref, out_ref):
    trials = trial_ref.shape[0]
    half = own_ref.shape[1] // 2
    out_ref[:trials, :] = jnp.dot(trial_ref[...], spread_ref[...], precision=lax.Precision.HIGHEST, preferred_element_type=F32)
    row = lax.broadcasted_iota(jnp.int32, (half, half), 0)
    column = lax.broadcasted_iota(jnp.int32, (half, half), 1)
    a, b, _, d = quads(own_ref[0], half)
    squares = [jnp.where(row <= column, a, d), b] + quads(beside_ref[0], half) + quads(across_ref[0], half)
    for i, square in enumerate(squares):
        start = trials + i * half
        out_ref[start : start + half, :] = square
    line = jnp.sum(jnp.where(row == column, d, 0.0), axis=0, keepdims=True)
    start = trials + len(squares) * half
    out_ref[start:, :] = jnp.broadcast_to(line, (out_ref.shape[0] - start, half))


def pack(ka, trials, spread, screened, parts):
    own = screened.shape[1] // parts
    half = own // 2

    def block(i):
        return pl.BlockSpec((1, own, own), lambda g, y: (0, (y[0] + i) % parts, y[0]))

    rows = trials.shape[0] + 10 * half + 8
    return pl.pallas_call(
        pack_body,
        out_shape=jax.ShapeDtypeStruct((rows, half), F32),
        grid_spec=pltpu.PrefetchScalarGridSpec(
            num_scalar_prefetch=1,
            grid=(1,),
            in_specs=[
                pl.BlockSpec(trials.shape, lambda g, y: (0, 0)),
                pl.BlockSpec(spread.shape, lambda g, y: (0, 0)),
                block(0),
                block(1),
                block(2),
            ],
            out_specs=pl.BlockSpec((rows, half), lambda g, y: (0, 0)),
        ),
    )(ka, trials, spread, screened, screened, screened)


def prepare_body(ka_ref, *refs):
    parts = len(refs) // 3 - 1
    conduct_ref, conduct_next_ref, rows_ref, joined_ref = refs[3 * parts :]
    each, width = refs[0].shape[1:]
    for i in range(3):
        for k in range(parts):
            place = pl.multiple_of(lax.rem(ka_ref[0] + parts - k, parts) * each, each)
            high, low = split(refs[i * parts + k][0])
            rows_ref[0, pl.ds(place, each), i * width : (i + 1) * width] = high
            rows_ref[0, pl.ds(parts * each + place, each), i * width : (i + 1) * width] = low
    joined_ref[0, :, :width] = conduct_ref[0]
    joined_ref[0, :, width:] = conduct_next_ref[0].astype(BF16)


def prepare(ka, valence, conduction, conduction_next):
    pairs, rows, waves = valence[0].shape
    parts = len(valence)
    own = waves // parts
    columns = conduction.shape[1]

    def column(i):
        return pl.BlockSpec((1, rows, own), lambda p, y: (p, 0, (y[0] + i) % parts))

    conduct = pl.BlockSpec((1, columns, own), lambda p, y: (p, 0, 0))
    shapes = (pairs, 2 * parts * rows, 3 * own), (pairs, columns, 2 * own)
    return pl.pallas_call(
        prepare_body,
        out_shape=tuple(jax.ShapeDtypeStruct(shape, BF16) for shape in shapes),
        grid_spec=pltpu.PrefetchScalarGridSpec(
            num_scalar_prefetch=1,
            grid=(pairs,),
            in_specs=[column(i) for i in range(3) for _ in range(parts)] + [conduct, conduct],
            out_specs=tuple(pl.BlockSpec((1,) + shape[1:], lambda p, y: (p, 0, 0)) for shape in shapes),
        ),
        cost_estimate=pl.CostEstimate(flops=0, bytes_accessed=pairs * rows * waves * 40, transcendentals=0),
    )(ka, *(valence * 3), conduction, conduction_next)


def one_pair(rows, blocks, conduct, out_ref, number, low_ref, high_ref, skip):
    half = blocks.shape[1]
    width = 2 * half
    count = rows.shape[0] // 2
    squares = [blocks[skip + i * half : skip + (i + 1) * half] for i in range(10)]
    line = blocks[skip + 10 * half : skip + 10 * half + 1]
    row = lax.broadcasted_iota(jnp.int32, (half, half), 0)
    column = lax.broadcasted_iota(jnp.int32, (half, half), 1)
    shared, corner = squares[:2]
    turned = shared.T
    a = jnp.where(row <= column, shared, turned)
    d = jnp.where(row > column, shared, jnp.where(row == column, line, turned))
    left = jnp.concatenate([a, corner.T, squares[2], squares[4], squares[6], squares[8]], axis=0)
    right = jnp.concatenate([corner, d, squares[3], squares[5], squares[7], squares[9]], axis=0)
    high, low = split(jnp.concatenate([left, right], axis=1))
    both = mul(rows, high, PLAIN)
    here = both[:count] + both[count:] + mul(rows[:count], low, PLAIN)
    both = mul(rows[:, :width], high[width : 2 * width], TURNED)
    there = both[:count] + both[count:] + mul(rows[:count, :width], low[width : 2 * width], TURNED)
    high, low = split(jnp.concatenate([here, there], axis=1))
    both = mul(jnp.concatenate([high, low], axis=0), conduct, TURNED)
    kernel = both[:count] + both[count:]
    low_ref[...] = kernel[:, :VC]
    high_ref[...] = jnp.concatenate([kernel[:, VC:], jnp.zeros((count, 2 * VC - kernel.shape[1]), F32)], axis=1)
    group = lax.broadcasted_iota(jnp.int32, (VB, VC), 1) // CD
    for part, ref in enumerate((low_ref, high_ref)):
        tiles = [ref[pl.ds(w, VB, stride=VB), :] for w in range(VB)]
        for step in (4, 2, 1):
            upper = (group & step) != 0
            for i in range(VB):
                if i & step:
                    continue
                a, b = tiles[i], tiles[i + step]
                tiles[i] = jnp.where(upper, pltpu.roll(b, step * CD, axis=1), a)
                tiles[i + step] = jnp.where(upper, b, pltpu.roll(a, VC - step * CD, axis=1))
        for i in range(VB):
            c = part * VB + i
            if c < CB:
                out_ref[number, c * VB : (c + 1) * VB, :] = tiles[i]


def pair_body(skip, momentum_ref, rows_ref, *refs):
    blocks, (conduct_ref, out_ref), scratch = refs[:PAIR], refs[PAIR : PAIR + 2], refs[PAIR + 2 :]
    for i in range(PAIR):
        one_pair(rows_ref[i], blocks[i][0], conduct_ref[i], out_ref, i, scratch[2 * i], scratch[2 * i + 1], skip)


def pair_kernels(start, count, momentum, rows, blocks, conduct, skip):
    first = start // PAIR

    def block(i):
        return pl.BlockSpec((1,) + blocks.shape[1:], lambda p, q: (q[start + PAIR * p + i], 0, 0))

    return pl.pallas_call(
        lambda *refs: pair_body(skip, *refs),
        out_shape=jax.ShapeDtypeStruct((count, VB * CB, VC), F32),
        grid_spec=pltpu.PrefetchScalarGridSpec(
            num_scalar_prefetch=1,
            grid=(count // PAIR,),
            in_specs=[pl.BlockSpec((PAIR,) + rows.shape[1:], lambda p, q: (first + p, 0, 0))]
            + [block(i) for i in range(PAIR)]
            + [pl.BlockSpec((PAIR,) + conduct.shape[1:], lambda p, q: (first + p, 0, 0))],
            out_specs=pl.BlockSpec((PAIR, VB * CB, VC), lambda p, q: (p, 0, 0)),
            scratch_shapes=[pltpu.VMEM((VB * VB, VC), F32)] * (2 * PAIR),
        ),
        cost_estimate=pl.CostEstimate(flops=count * 10**8, bytes_accessed=count * 11 * 10**5, transcendentals=0),
    )(momentum, rows, *([blocks] * PAIR), conduct)


def response_body(start, counts, near_ref, far_ref, near_place_ref, far_place_ref, trial_ref, *refs):
    kernels, (out_ref, turn_ref) = refs[: len(counts)], refs[-2:]
    if len(refs) > len(counts) + 2:
        out_ref[...] = refs[len(counts)][...]
    else:
        out_ref[...] = jnp.zeros_like(out_ref)
    turn_ref[...] = jnp.zeros_like(turn_ref)
    for count, kernel_ref in zip(counts, kernels):

        @pl.loop(0, count)
        def _(p, start=start, kernel_ref=kernel_ref):
            near, far = near_ref[start + p], far_ref[start + p]
            for v in range(VB):
                turn_ref[v * CD : v * CD + CB, :] = kernel_ref[p, pl.ds(v, CB, stride=VB), :]
            kernel = turn_ref[...]
            direct = mul3(trial_ref[far], kernel, TURNED)
            mirror = mul3(trial_ref[near], kernel, PLAIN)
            near, far = near_place_ref[start + p], far_place_ref[start + p]
            out_ref[near] = out_ref[near] + direct
            out_ref[far] = out_ref[far] + mirror

        start += count


def contributions(start, places, blocks, trials, kernels, before=()):
    counts = [kernel.shape[0] for kernel in kernels]
    shape = (blocks.shape[0], trials, VC)
    whole = [pl.BlockSpec(x.shape, lambda g: (0, 0, 0)) for x in kernels]
    result = pl.BlockSpec(shape, lambda g: (0, 0, 0))
    scalar = pl.BlockSpec(memory_space=pltpu.SMEM)
    return pl.pallas_call(
        lambda *refs: response_body(start, counts, *refs),
        out_shape=jax.ShapeDtypeStruct(shape, F32),
        grid=(1,),
        in_specs=[scalar] * len(places) + [result, *whole] + [result] * len(before),
        out_specs=result,
        scratch_shapes=[pltpu.VMEM((VC, VC), F32)],
        cost_estimate=pl.CostEstimate(flops=sum(counts) * 10**7, bytes_accessed=4 * 10**6, transcendentals=0),
    )(*places, blocks, *kernels, *before)


def compute(valence, conduction, screened, momentum, kpairs, kpoint_slot, trial_blocks):
    ka = lax.axis_size("ka")
    pair_dev = valence.shape[0]
    own = conduction.shape[2]
    here = lax.axis_index("ka").astype(jnp.int32).reshape(1)
    own_trials = trial_blocks.reshape(-1, VB * CB)
    local_trials = own_trials.shape[0]
    entry = np.arange(VB * CB)
    spread = np.zeros((VB * CB, VC), np.float32)
    spread[entry, entry // CB * CD + entry % CB] = 1.0
    blocks = lax.all_gather(pack(here, own_trials, jnp.asarray(spread), screened, ka), "pb")

    ahead = [(i, (i + 1) % ka) for i in range(ka)]
    back = [((i + 1) % ka, i) for i in range(ka)]
    conduct = conduction.reshape(pair_dev, CB, CB, own)
    conduct = jnp.pad(conduct, ((0, 0), (0, 0), (0, CD - CB), (0, 0))).reshape(pair_dev, CB * CD, own)
    conduct_next = lax.ppermute(conduct.astype(F32), "ka", back)
    rows = [valence]
    for _ in range(ka - 1):
        rows.append(lax.ppermute(rows[-1], "ka", ahead))
    near = jnp.take(kpoint_slot, kpairs[:, 0])
    far = jnp.take(kpoint_slot, kpairs[:, 1])
    rows, conduct = prepare(here, rows, conduct, conduct_next)
    owners = lax.axis_size("pb")
    core = lax.rem(lax.axis_index("pb").astype(jnp.int32), 2)
    places = [near, far] + [lax.rem(x + core, 2) * (owners // 2) + x // 2 for x in (near, far)]
    rows, conduct, places = lax.optimization_barrier((rows, conduct, places))

    swap = [(i, i ^ 1) for i in range(ka)]
    fold = [(i, ka - 1 - i) for i in range(ka)]
    target = momentum[:, 0]
    each = max(PAIR, pair_dev // 4 // PAIR * PAIR)
    sizes = [pair_dev - 3 * each, each, each, each]
    turns = (swap, fold)

    def again(i, kernel):
        return kernel + lax.ppermute(kernel, "ka", turns[1 - i % 2])

    kernels, start = [], 0
    for i, size in enumerate(sizes):
        if i == len(sizes) - 1:
            target, kernels[0] = lax.optimization_barrier((target, kernels[0]))
            kernels[0] = again(0, kernels[0])
        kernel = pair_kernels(start, size, target, rows, blocks, conduct, local_trials)
        kernels.append(kernel + lax.ppermute(kernel, "ka", turns[i % 2]))
        start += size
    for i in range(1, len(sizes)):
        kernels[i] = again(i, kernels[i])

    summed = contributions(0, places, blocks, local_trials, kernels[:2])
    summed = contributions(sum(sizes[:2]), places, blocks, local_trials, kernels[2:], (summed,))
    half = owners // 2
    other = lax.ppermute(summed[half:], "pb", [(i, i ^ 1) for i in range(owners)])
    groups = [list(range(c, owners, 2)) for c in range(2)]
    parts = lax.all_to_all(summed[:half] + other, "pb", split_axis=0, concat_axis=0, axis_index_groups=groups, tiled=True)
    response = jnp.sum(parts, axis=0).reshape(local_trials, VB, CD)[:, :, :CB]
    return response.reshape(1, -1)


def solution(mesh):
    return jax.shard_map(
        compute,
        mesh=mesh,
        in_specs=(
            P("pb", "ka", None),
            P("pb", None, "ka"),
            P("pb", None, None),
            P("pb", None),
            P("pb", None),
            P(),
            P("pb", "ka"),
        ),
        out_specs=P("pb", "ka"),
        check_vma=False,
    )
```

```python
import jax
import jax.numpy as jnp
import numpy as np
from jax import lax
from jax.experimental import pallas as pl
from jax.experimental.pallas import tpu as pltpu
from jax.sharding import PartitionSpec as P

VB = 8
CB = 14
CD = 16
VC = VB * CD
PAIR = 2
F32 = jnp.float32
BF16 = jnp.bfloat16
PLAIN = ((1,), (0,))
TURNED = ((1,), (1,))


def split(x):
    high = x.astype(BF16)
    return high, (x - high.astype(F32)).astype(BF16)


def mul(a, b, dims):
    return lax.dot_general(a, b, (dims, ((), ())), preferred_element_type=F32)


def mul3(a, b, dims=PLAIN):
    rows = a.shape[0]
    a_high, a_low = split(a)
    b_high, b_low = split(b)
    both = mul(jnp.concatenate([a_high, a_low], axis=0), b_high, dims)
    return both[:rows] + both[rows:] + mul(a_high, b_low, dims)


def quads(x, half):
    return [x[i : i + half, j : j + half] for i in (0, half) for j in (0, half)]


def pack_body(ka_ref, trial_ref, spread_ref, own_ref, beside_ref, across_ref, out_ref):
    trials = trial_ref.shape[0]
    half = own_ref.shape[1] // 2
    out_ref[:trials, :] = jnp.dot(trial_ref[...], spread_ref[...], precision=lax.Precision.HIGHEST, preferred_element_type=F32)
    row = lax.broadcasted_iota(jnp.int32, (half, half), 0)
    column = lax.broadcasted_iota(jnp.int32, (half, half), 1)
    a, b, _, d = quads(own_ref[0], half)
    squares = [jnp.where(row <= column, a, d), b] + quads(beside_ref[0], half) + quads(across_ref[0], half)
    for i, square in enumerate(squares):
        start = trials + i * half
        out_ref[start : start + half, :] = square
    line = jnp.sum(jnp.where(row == column, d, 0.0), axis=0, keepdims=True)
    start = trials + len(squares) * half
    out_ref[start:, :] = jnp.broadcast_to(line, (out_ref.shape[0] - start, half))


def pack(ka, trials, spread, screened, parts):
    own = screened.shape[1] // parts
    half = own // 2

    def block(i):
        return pl.BlockSpec((1, own, own), lambda g, y: (0, (y[0] + i) % parts, y[0]))

    rows = trials.shape[0] + 10 * half + 8
    return pl.pallas_call(
        pack_body,
        out_shape=jax.ShapeDtypeStruct((rows, half), F32),
        grid_spec=pltpu.PrefetchScalarGridSpec(
            num_scalar_prefetch=1,
            grid=(1,),
            in_specs=[
                pl.BlockSpec(trials.shape, lambda g, y: (0, 0)),
                pl.BlockSpec(spread.shape, lambda g, y: (0, 0)),
                block(0),
                block(1),
                block(2),
            ],
            out_specs=pl.BlockSpec((rows, half), lambda g, y: (0, 0)),
        ),
    )(ka, trials, spread, screened, screened, screened)


def prepare_body(ka_ref, *refs):
    parts = len(refs) // 3 - 1
    conduct_ref, conduct_next_ref, rows_ref, joined_ref = refs[3 * parts :]
    each, width = refs[0].shape[1:]
    for i in range(3):
        for k in range(parts):
            place = pl.multiple_of(lax.rem(ka_ref[0] + parts - k, parts) * each, each)
            high, low = split(refs[i * parts + k][0])
            rows_ref[0, pl.ds(place, each), i * width : (i + 1) * width] = high
            rows_ref[0, pl.ds(parts * each + place, each), i * width : (i + 1) * width] = low
    joined_ref[0, :, :width] = conduct_ref[0]
    joined_ref[0, :, width:] = conduct_next_ref[0].astype(BF16)


def prepare(ka, valence, conduction, conduction_next):
    pairs, rows, waves = valence[0].shape
    parts = len(valence)
    own = waves // parts
    columns = conduction.shape[1]

    def column(i):
        return pl.BlockSpec((1, rows, own), lambda p, y: (p, 0, (y[0] + i) % parts))

    conduct = pl.BlockSpec((1, columns, own), lambda p, y: (p, 0, 0))
    shapes = (pairs, 2 * parts * rows, 3 * own), (pairs, columns, 2 * own)
    return pl.pallas_call(
        prepare_body,
        out_shape=tuple(jax.ShapeDtypeStruct(shape, BF16) for shape in shapes),
        grid_spec=pltpu.PrefetchScalarGridSpec(
            num_scalar_prefetch=1,
            grid=(pairs,),
            in_specs=[column(i) for i in range(3) for _ in range(parts)] + [conduct, conduct],
            out_specs=tuple(pl.BlockSpec((1,) + shape[1:], lambda p, y: (p, 0, 0)) for shape in shapes),
        ),
        cost_estimate=pl.CostEstimate(flops=0, bytes_accessed=pairs * rows * waves * 40, transcendentals=0),
    )(ka, *(valence * 3), conduction, conduction_next)


def one_pair(rows, blocks, conduct, out_ref, low_ref, high_ref, skip):
    half = blocks.shape[1]
    width = 2 * half
    count = rows.shape[0] // 2
    squares = [blocks[skip + i * half : skip + (i + 1) * half] for i in range(10)]
    line = blocks[skip + 10 * half : skip + 10 * half + 1]
    row = lax.broadcasted_iota(jnp.int32, (half, half), 0)
    column = lax.broadcasted_iota(jnp.int32, (half, half), 1)
    shared, corner = squares[:2]
    turned = shared.T
    a = jnp.where(row <= column, shared, turned)
    d = jnp.where(row > column, shared, jnp.where(row == column, line, turned))
    left = jnp.concatenate([a, corner.T, squares[2], squares[4], squares[6], squares[8]], axis=0)
    right = jnp.concatenate([corner, d, squares[3], squares[5], squares[7], squares[9]], axis=0)
    high, low = split(jnp.concatenate([left, right], axis=1))
    both = mul(rows, high, PLAIN)
    here = both[:count] + both[count:] + mul(rows[:count], low, PLAIN)
    both = mul(rows[:, :width], high[width : 2 * width], TURNED)
    there = both[:count] + both[count:] + mul(rows[:count, :width], low[width : 2 * width], TURNED)
    high, low = split(jnp.concatenate([here, there], axis=1))
    both = mul(jnp.concatenate([high, low], axis=0), conduct, TURNED)
    kernel = both[:count] + both[count:]
    low_ref[...] = kernel[:, :VC]
    high_ref[...] = jnp.concatenate([kernel[:, VC:], jnp.zeros((count, 2 * VC - kernel.shape[1]), F32)], axis=1)
    group = lax.broadcasted_iota(jnp.int32, (VB, VC), 1) // CD
    for part, ref in enumerate((low_ref, high_ref)):
        tiles = [ref[pl.ds(w, VB, stride=VB), :] for w in range(VB)]
        for step in (4, 2, 1):
            upper = (group & step) != 0
            for i in range(VB):
                if i & step:
                    continue
                a, b = tiles[i], tiles[i + step]
                tiles[i] = jnp.where(upper, pltpu.roll(b, step * CD, axis=1), a)
                tiles[i + step] = jnp.where(upper, b, pltpu.roll(a, VC - step * CD, axis=1))
        for i in range(VB):
            c = part * VB + i
            if c < CB:
                out_ref[0, c * VB : (c + 1) * VB, :] = tiles[i]


def pair_body(skip, momentum_ref, rows_ref, *refs):
    blocks, conduct_ref, outs, scratch = refs[:PAIR], refs[PAIR], refs[PAIR + 1 : 2 * PAIR + 1], refs[2 * PAIR + 1 :]
    for i in range(PAIR):
        one_pair(rows_ref[i], blocks[i][0], conduct_ref[i], outs[i], scratch[2 * i], scratch[2 * i + 1], skip)


def pair_kernels(start, count, momentum, rows, blocks, conduct, skip):
    first = start // PAIR

    def block(i):
        return pl.BlockSpec((1,) + blocks.shape[1:], lambda p, q: (q[start + PAIR * p + i], 0, 0))

    return pl.pallas_call(
        lambda *refs: pair_body(skip, *refs),
        out_shape=[jax.ShapeDtypeStruct((count // PAIR, VB * CB, VC), F32)] * PAIR,
        grid_spec=pltpu.PrefetchScalarGridSpec(
            num_scalar_prefetch=1,
            grid=(count // PAIR,),
            in_specs=[pl.BlockSpec((PAIR,) + rows.shape[1:], lambda p, q: (first + p, 0, 0))]
            + [block(i) for i in range(PAIR)]
            + [pl.BlockSpec((PAIR,) + conduct.shape[1:], lambda p, q: (first + p, 0, 0))],
            out_specs=[pl.BlockSpec((1, VB * CB, VC), lambda p, q: (p, 0, 0))] * PAIR,
            scratch_shapes=[pltpu.VMEM((VB * VB, VC), F32)] * (2 * PAIR),
        ),
        cost_estimate=pl.CostEstimate(flops=count * 10**8, bytes_accessed=count * 11 * 10**5, transcendentals=0),
    )(momentum, rows, *([blocks] * PAIR), conduct)


def response_body(start, counts, near_ref, far_ref, near_place_ref, far_place_ref, trial_ref, *refs):
    kernels, (out_ref, turn_ref) = refs[: len(counts)], refs[-2:]
    if len(refs) > len(counts) + 2:
        out_ref[...] = refs[len(counts)][...]
    else:
        out_ref[...] = jnp.zeros_like(out_ref)
    turn_ref[...] = jnp.zeros_like(turn_ref)
    for number, (count, kernel_ref) in enumerate(zip(counts, kernels)):

        @pl.loop(0, count)
        def _(p, number=number, kernel_ref=kernel_ref):
            pair = start + PAIR * p + number
            near, far = near_ref[pair], far_ref[pair]
            for v in range(VB):
                turn_ref[v * CD : v * CD + CB, :] = kernel_ref[p, pl.ds(v, CB, stride=VB), :]
            kernel = turn_ref[...]
            direct = mul3(trial_ref[far], kernel, TURNED)
            mirror = mul3(trial_ref[near], kernel, PLAIN)
            near, far = near_place_ref[pair], far_place_ref[pair]
            out_ref[near] = out_ref[near] + direct
            out_ref[far] = out_ref[far] + mirror


def contributions(start, places, blocks, trials, kernels, before=()):
    counts = [kernel.shape[0] for kernel in kernels]
    shape = (blocks.shape[0], trials, VC)
    whole = [pl.BlockSpec(x.shape, lambda g: (0, 0, 0)) for x in kernels]
    result = pl.BlockSpec(shape, lambda g: (0, 0, 0))
    scalar = pl.BlockSpec(memory_space=pltpu.SMEM)
    return pl.pallas_call(
        lambda *refs: response_body(start, counts, *refs),
        out_shape=jax.ShapeDtypeStruct(shape, F32),
        grid=(1,),
        in_specs=[scalar] * len(places) + [result, *whole] + [result] * len(before),
        out_specs=result,
        scratch_shapes=[pltpu.VMEM((VC, VC), F32)],
        cost_estimate=pl.CostEstimate(flops=sum(counts) * 10**7, bytes_accessed=4 * 10**6, transcendentals=0),
    )(*places, blocks, *kernels, *before)


def compute(valence, conduction, screened, momentum, kpairs, kpoint_slot, trial_blocks):
    ka = lax.axis_size("ka")
    pair_dev = valence.shape[0]
    own = conduction.shape[2]
    here = lax.axis_index("ka").astype(jnp.int32).reshape(1)
    own_trials = trial_blocks.reshape(-1, VB * CB)
    local_trials = own_trials.shape[0]
    entry = np.arange(VB * CB)
    spread = np.zeros((VB * CB, VC), np.float32)
    spread[entry, entry // CB * CD + entry % CB] = 1.0
    blocks = lax.all_gather(pack(here, own_trials, jnp.asarray(spread), screened, ka), "pb")

    ahead = [(i, (i + 1) % ka) for i in range(ka)]
    back = [((i + 1) % ka, i) for i in range(ka)]
    conduct = conduction.reshape(pair_dev, CB, CB, own)
    conduct = jnp.pad(conduct, ((0, 0), (0, 0), (0, CD - CB), (0, 0))).reshape(pair_dev, CB * CD, own)
    conduct_next = lax.ppermute(conduct.astype(F32), "ka", back)
    rows = [valence]
    for _ in range(ka - 1):
        rows.append(lax.ppermute(rows[-1], "ka", ahead))
    near = jnp.take(kpoint_slot, kpairs[:, 0])
    far = jnp.take(kpoint_slot, kpairs[:, 1])
    rows, conduct = prepare(here, rows, conduct, conduct_next)
    owners = lax.axis_size("pb")
    core = lax.rem(lax.axis_index("pb").astype(jnp.int32), 2)
    places = [near, far] + [lax.rem(x + core, 2) * (owners // 2) + x // 2 for x in (near, far)]
    rows, conduct, places = lax.optimization_barrier((rows, conduct, places))

    swap = [(i, i ^ 1) for i in range(ka)]
    fold = [(i, ka - 1 - i) for i in range(ka)]
    target = momentum[:, 0]
    turns = (swap, fold)
    cut = -(-pair_dev // (2 * PAIR)) * PAIR

    def exchanged(number, first):
        return [x + lax.ppermute(x, "ka", turns[(i + number) % 2]) for i, x in enumerate(first)]

    first = pair_kernels(0, cut, target, rows, blocks, conduct, local_trials)
    first = exchanged(0, first)
    second = pair_kernels(cut, pair_dev - cut, target, rows, blocks, conduct, local_trials)
    first = exchanged(1, first)
    second = exchanged(0, second)
    second = exchanged(1, second)
    summed = contributions(0, places, blocks, local_trials, first)
    summed = contributions(cut, places, blocks, local_trials, second, (summed,))
    half = owners // 2
    other = lax.ppermute(summed[half:], "pb", [(i, i ^ 1) for i in range(owners)])
    groups = [list(range(c, owners, 2)) for c in range(2)]
    parts = lax.all_to_all(summed[:half] + other, "pb", split_axis=0, concat_axis=0, axis_index_groups=groups, tiled=True)
    response = jnp.sum(parts, axis=0).reshape(local_trials, VB, CD)[:, :, :CB]
    return response.reshape(1, -1)


def solution(mesh):
    return jax.shard_map(
        compute,
        mesh=mesh,
        in_specs=(
            P("pb", "ka", None),
            P("pb", None, "ka"),
            P("pb", None, None),
            P("pb", None),
            P("pb", None),
            P(),
            P("pb", "ka"),
        ),
        out_specs=P("pb", "ka"),
        check_vma=False,
    )
```

```python
import jax
import jax.numpy as jnp
import numpy as np
from jax import lax
from jax.experimental import pallas as pl
from jax.experimental.pallas import tpu as pltpu
from jax.sharding import PartitionSpec as P

VB = 8
CB = 14
CD = 16
VC = VB * CD
PAIR = 2
F32 = jnp.float32
BF16 = jnp.bfloat16
PLAIN = ((1,), (0,))
TURNED = ((1,), (1,))


def split(x):
    high = x.astype(BF16)
    return high, (x - high.astype(F32)).astype(BF16)


def mul(a, b, dims):
    return lax.dot_general(a, b, (dims, ((), ())), preferred_element_type=F32)


def mul3(a, b, dims=PLAIN):
    rows = a.shape[0]
    a_high, a_low = split(a)
    b_high, b_low = split(b)
    both = mul(jnp.concatenate([a_high, a_low], axis=0), b_high, dims)
    return both[:rows] + both[rows:] + mul(a_high, b_low, dims)


def quads(x, half):
    return [x[i : i + half, j : j + half] for i in (0, half) for j in (0, half)]


def pack_body(ka_ref, trial_ref, spread_ref, own_ref, beside_ref, across_ref, out_ref):
    trials = trial_ref.shape[0]
    half = own_ref.shape[1] // 2
    out_ref[:trials, :] = jnp.dot(trial_ref[...], spread_ref[...], precision=lax.Precision.HIGHEST, preferred_element_type=F32)
    row = lax.broadcasted_iota(jnp.int32, (half, half), 0)
    column = lax.broadcasted_iota(jnp.int32, (half, half), 1)
    a, b, _, d = quads(own_ref[0], half)
    squares = [jnp.where(row <= column, a, d), b] + quads(beside_ref[0], half) + quads(across_ref[0], half)
    for i, square in enumerate(squares):
        start = trials + i * half
        out_ref[start : start + half, :] = square
    line = jnp.sum(jnp.where(row == column, d, 0.0), axis=0, keepdims=True)
    start = trials + len(squares) * half
    out_ref[start:, :] = jnp.broadcast_to(line, (out_ref.shape[0] - start, half))


def pack(ka, trials, spread, screened, parts):
    own = screened.shape[1] // parts
    half = own // 2

    def block(i):
        return pl.BlockSpec((1, own, own), lambda g, y: (0, (y[0] + i) % parts, y[0]))

    rows = trials.shape[0] + 10 * half + 8
    return pl.pallas_call(
        pack_body,
        out_shape=jax.ShapeDtypeStruct((rows, half), F32),
        grid_spec=pltpu.PrefetchScalarGridSpec(
            num_scalar_prefetch=1,
            grid=(1,),
            in_specs=[
                pl.BlockSpec(trials.shape, lambda g, y: (0, 0)),
                pl.BlockSpec(spread.shape, lambda g, y: (0, 0)),
                block(0),
                block(1),
                block(2),
            ],
            out_specs=pl.BlockSpec((rows, half), lambda g, y: (0, 0)),
        ),
    )(ka, trials, spread, screened, screened, screened)


def prepare_body(ka_ref, *refs):
    parts = len(refs) // 3 - 1
    conduct_ref, conduct_next_ref, rows_ref, joined_ref = refs[3 * parts :]
    each, width = refs[0].shape[1:]
    for i in range(3):
        for k in range(parts):
            place = pl.multiple_of(lax.rem(ka_ref[0] + parts - k, parts) * each, each)
            high, low = split(refs[i * parts + k][0])
            rows_ref[0, pl.ds(place, each), i * width : (i + 1) * width] = high
            rows_ref[0, pl.ds(parts * each + place, each), i * width : (i + 1) * width] = low
    joined_ref[0, :, :width] = conduct_ref[0]
    joined_ref[0, :, width:] = conduct_next_ref[0].astype(BF16)


def prepare(ka, valence, conduction, conduction_next):
    pairs, rows, waves = valence[0].shape
    parts = len(valence)
    own = waves // parts
    columns = conduction.shape[1]

    def column(i):
        return pl.BlockSpec((1, rows, own), lambda p, y: (p, 0, (y[0] + i) % parts))

    conduct = pl.BlockSpec((1, columns, own), lambda p, y: (p, 0, 0))
    shapes = (pairs, 2 * parts * rows, 3 * own), (pairs, columns, 2 * own)
    return pl.pallas_call(
        prepare_body,
        out_shape=tuple(jax.ShapeDtypeStruct(shape, BF16) for shape in shapes),
        grid_spec=pltpu.PrefetchScalarGridSpec(
            num_scalar_prefetch=1,
            grid=(pairs,),
            in_specs=[column(i) for i in range(3) for _ in range(parts)] + [conduct, conduct],
            out_specs=tuple(pl.BlockSpec((1,) + shape[1:], lambda p, y: (p, 0, 0)) for shape in shapes),
        ),
        cost_estimate=pl.CostEstimate(flops=0, bytes_accessed=pairs * rows * waves * 40, transcendentals=0),
    )(ka, *(valence * 3), conduction, conduction_next)


def one_pair(rows, blocks, conduct, out_ref, low_ref, high_ref, skip):
    half = blocks.shape[1]
    width = 2 * half
    count = rows.shape[0] // 2
    squares = [blocks[skip + i * half : skip + (i + 1) * half] for i in range(10)]
    line = blocks[skip + 10 * half : skip + 10 * half + 1]
    row = lax.broadcasted_iota(jnp.int32, (half, half), 0)
    column = lax.broadcasted_iota(jnp.int32, (half, half), 1)
    shared, corner = squares[:2]
    turned = shared.T
    a = jnp.where(row <= column, shared, turned)
    d = jnp.where(row > column, shared, jnp.where(row == column, line, turned))
    left = jnp.concatenate([a, corner.T, squares[2], squares[4], squares[6], squares[8]], axis=0)
    right = jnp.concatenate([corner, d, squares[3], squares[5], squares[7], squares[9]], axis=0)
    high, low = split(jnp.concatenate([left, right], axis=1))
    both = mul(rows, high, PLAIN)
    here = both[:count] + both[count:] + mul(rows[:count], low, PLAIN)
    both = mul(rows[:, :width], high[width : 2 * width], TURNED)
    there = both[:count] + both[count:] + mul(rows[:count, :width], low[width : 2 * width], TURNED)
    high, low = split(jnp.concatenate([here, there], axis=1))
    both = mul(jnp.concatenate([high, low], axis=0), conduct, TURNED)
    kernel = both[:count] + both[count:]
    low_ref[...] = kernel[:, :VC]
    high_ref[...] = jnp.concatenate([kernel[:, VC:], jnp.zeros((count, 2 * VC - kernel.shape[1]), F32)], axis=1)
    group = lax.broadcasted_iota(jnp.int32, (VB, VC), 1) // CD
    for part, ref in enumerate((low_ref, high_ref)):
        tiles = [ref[pl.ds(w, VB, stride=VB), :] for w in range(VB)]
        for step in (4, 2, 1):
            upper = (group & step) != 0
            for i in range(VB):
                if i & step:
                    continue
                a, b = tiles[i], tiles[i + step]
                tiles[i] = jnp.where(upper, pltpu.roll(b, step * CD, axis=1), a)
                tiles[i + step] = jnp.where(upper, b, pltpu.roll(a, VC - step * CD, axis=1))
        for i in range(VB):
            c = part * VB + i
            if c < CB:
                out_ref[0, c * VB : (c + 1) * VB, :] = tiles[i]


def pair_body(skip, momentum_ref, rows_ref, *refs):
    blocks, conduct_ref, outs, scratch = refs[:PAIR], refs[PAIR], refs[PAIR + 1 : 2 * PAIR + 1], refs[2 * PAIR + 1 :]
    for i in range(PAIR):
        one_pair(rows_ref[i], blocks[i][0], conduct_ref[i], outs[i], scratch[2 * i], scratch[2 * i + 1], skip)


def pair_kernels(start, count, momentum, rows, blocks, conduct, skip):
    first = start // PAIR

    def block(i):
        return pl.BlockSpec((1,) + blocks.shape[1:], lambda p, q: (q[start + PAIR * p + i], 0, 0))

    return pl.pallas_call(
        lambda *refs: pair_body(skip, *refs),
        out_shape=[jax.ShapeDtypeStruct((count // PAIR, VB * CB, VC), F32)] * PAIR,
        grid_spec=pltpu.PrefetchScalarGridSpec(
            num_scalar_prefetch=1,
            grid=(count // PAIR,),
            in_specs=[pl.BlockSpec((PAIR,) + rows.shape[1:], lambda p, q: (first + p, 0, 0))]
            + [block(i) for i in range(PAIR)]
            + [pl.BlockSpec((PAIR,) + conduct.shape[1:], lambda p, q: (first + p, 0, 0))],
            out_specs=[pl.BlockSpec((1, VB * CB, VC), lambda p, q: (p, 0, 0))] * PAIR,
            scratch_shapes=[pltpu.VMEM((VB * VB, VC), F32)] * (2 * PAIR),
        ),
        cost_estimate=pl.CostEstimate(flops=count * 10**8, bytes_accessed=count * 11 * 10**5, transcendentals=0),
    )(momentum, rows, *([blocks] * PAIR), conduct)


def response_body(bases, near_ref, far_ref, near_place_ref, far_place_ref, trial_ref, *refs):
    kernels, (out_ref, turn_ref) = refs[: 2 * len(bases)], refs[-2:]
    if len(refs) > 2 * len(bases) + 2:
        out_ref[...] = refs[2 * len(bases)][...]
    else:
        out_ref[...] = jnp.zeros_like(out_ref)
    turn_ref[...] = jnp.zeros_like(turn_ref)
    for number, base in enumerate(bases):
        own_ref, came_ref = kernels[2 * number : 2 * number + 2]

        @pl.loop(0, own_ref.shape[0])
        def _(p, base=base, own_ref=own_ref, came_ref=came_ref):
            pair = base + PAIR * p
            near, far = near_ref[pair], far_ref[pair]
            for v in range(VB):
                rows = pl.ds(v, CB, stride=VB)
                turn_ref[v * CD : v * CD + CB, :] = own_ref[p, rows, :] + came_ref[p, rows, :]
            kernel = turn_ref[...]
            direct = mul3(trial_ref[far], kernel, TURNED)
            mirror = mul3(trial_ref[near], kernel, PLAIN)
            near, far = near_place_ref[pair], far_place_ref[pair]
            out_ref[near] = out_ref[near] + direct
            out_ref[far] = out_ref[far] + mirror


def contributions(bases, places, blocks, trials, kernels, before=()):
    pairs = sum(kernel.shape[0] for kernel in kernels) // 2
    shape = (blocks.shape[0], trials, VC)
    whole = [pl.BlockSpec(x.shape, lambda g: (0, 0, 0)) for x in kernels]
    result = pl.BlockSpec(shape, lambda g: (0, 0, 0))
    scalar = pl.BlockSpec(memory_space=pltpu.SMEM)
    return pl.pallas_call(
        lambda *refs: response_body(bases, *refs),
        out_shape=jax.ShapeDtypeStruct(shape, F32),
        grid=(1,),
        in_specs=[scalar] * len(places) + [result, *whole] + [result] * len(before),
        out_specs=result,
        scratch_shapes=[pltpu.VMEM((VC, VC), F32)],
        cost_estimate=pl.CostEstimate(flops=pairs * 10**7, bytes_accessed=4 * 10**6, transcendentals=0),
    )(*places, blocks, *kernels, *before)


def compute(valence, conduction, screened, momentum, kpairs, kpoint_slot, trial_blocks):
    ka = lax.axis_size("ka")
    pair_dev = valence.shape[0]
    own = conduction.shape[2]
    here = lax.axis_index("ka").astype(jnp.int32).reshape(1)
    own_trials = trial_blocks.reshape(-1, VB * CB)
    local_trials = own_trials.shape[0]
    entry = np.arange(VB * CB)
    spread = np.zeros((VB * CB, VC), np.float32)
    spread[entry, entry // CB * CD + entry % CB] = 1.0
    blocks = lax.all_gather(pack(here, own_trials, jnp.asarray(spread), screened, ka), "pb")

    ahead = [(i, (i + 1) % ka) for i in range(ka)]
    back = [((i + 1) % ka, i) for i in range(ka)]
    conduct = conduction.reshape(pair_dev, CB, CB, own)
    conduct = jnp.pad(conduct, ((0, 0), (0, 0), (0, CD - CB), (0, 0))).reshape(pair_dev, CB * CD, own)
    conduct_next = lax.ppermute(conduct.astype(F32), "ka", back)
    rows = [valence]
    for _ in range(ka - 1):
        rows.append(lax.ppermute(rows[-1], "ka", ahead))
    near = jnp.take(kpoint_slot, kpairs[:, 0])
    far = jnp.take(kpoint_slot, kpairs[:, 1])
    rows, conduct = prepare(here, rows, conduct, conduct_next)
    owners = lax.axis_size("pb")
    core = lax.rem(lax.axis_index("pb").astype(jnp.int32), 2)
    places = [near, far] + [lax.rem(x + core, 2) * (owners // 2) + x // 2 for x in (near, far)]
    rows, conduct, places = lax.optimization_barrier((rows, conduct, places))

    swap = [(i, i ^ 1) for i in range(ka)]
    fold = [(i, ka - 1 - i) for i in range(ka)]
    target = momentum[:, 0]
    turns = (swap, fold)
    each = -(-3 * pair_dev // (8 * PAIR)) * PAIR
    starts = [0, each, 2 * each]
    sizes = [each, each, pair_dev - 2 * each]

    def twice(kernels):
        came = [lax.ppermute(x, "ka", turns[1 - i % 2]) for i, x in enumerate(kernels)]
        return [x for both in zip(kernels, came) for x in both]

    calls = []
    for call in range(3):
        kernels = pair_kernels(starts[call], sizes[call], target, rows, blocks, conduct, local_trials)
        calls.append([x + lax.ppermute(x, "ka", turns[i % 2]) for i, x in enumerate(kernels)])
    calls = [twice(kernels) for kernels in calls]
    bases = [[start + i for i in range(PAIR)] for start in starts]
    summed = contributions(bases[0] + bases[1], places, blocks, local_trials, calls[0] + calls[1])
    summed = contributions(bases[2], places, blocks, local_trials, calls[2], (summed,))
    half = owners // 2
    other = lax.ppermute(summed[half:], "pb", [(i, i ^ 1) for i in range(owners)])
    groups = [list(range(c, owners, 2)) for c in range(2)]
    parts = lax.all_to_all(summed[:half] + other, "pb", split_axis=0, concat_axis=0, axis_index_groups=groups, tiled=True)
    response = jnp.sum(parts, axis=0).reshape(local_trials, VB, CD)[:, :, :CB]
    return response.reshape(1, -1)


def solution(mesh):
    return jax.shard_map(
        compute,
        mesh=mesh,
        in_specs=(
            P("pb", "ka", None),
            P("pb", None, "ka"),
            P("pb", None, None),
            P("pb", None),
            P("pb", None),
            P(),
            P("pb", "ka"),
        ),
        out_specs=P("pb", "ka"),
        check_vma=False,
    )
```

```python
import jax
import jax.numpy as jnp
import numpy as np
from jax import lax
from jax.experimental import pallas as pl
from jax.experimental.pallas import tpu as pltpu
from jax.sharding import PartitionSpec as P

VB = 8
CB = 14
CD = 16
VC = VB * CD
PAIR = 2
F32 = jnp.float32
BF16 = jnp.bfloat16
PLAIN = ((1,), (0,))
TURNED = ((1,), (1,))


def split(x):
    high = x.astype(BF16)
    return high, (x - high.astype(F32)).astype(BF16)


def mul(a, b, dims):
    return lax.dot_general(a, b, (dims, ((), ())), preferred_element_type=F32)


def mul3(a, b, dims=PLAIN):
    rows = a.shape[0]
    a_high, a_low = split(a)
    b_high, b_low = split(b)
    both = mul(jnp.concatenate([a_high, a_low], axis=0), b_high, dims)
    return both[:rows] + both[rows:] + mul(a_high, b_low, dims)


def quads(x, half):
    return [x[i : i + half, j : j + half] for i in (0, half) for j in (0, half)]


def pack_body(ka_ref, trial_ref, spread_ref, own_ref, beside_ref, across_ref, out_ref):
    trials = trial_ref.shape[1] // spread_ref.shape[0]
    half = own_ref.shape[1] // 2
    entries = spread_ref.shape[0]
    lines = jnp.concatenate([trial_ref[:, i * entries : (i + 1) * entries] for i in range(trials)], axis=0)
    out_ref[:trials, :] = jnp.dot(lines, spread_ref[...], precision=lax.Precision.HIGHEST, preferred_element_type=F32)
    row = lax.broadcasted_iota(jnp.int32, (half, half), 0)
    column = lax.broadcasted_iota(jnp.int32, (half, half), 1)
    a, b, _, d = quads(own_ref[0], half)
    squares = [jnp.where(row <= column, a, d), b] + quads(beside_ref[0], half) + quads(across_ref[0], half)
    for i, square in enumerate(squares):
        start = trials + i * half
        out_ref[start : start + half, :] = square
    line = jnp.sum(jnp.where(row == column, d, 0.0), axis=0, keepdims=True)
    start = trials + len(squares) * half
    out_ref[start:, :] = jnp.broadcast_to(line, (out_ref.shape[0] - start, half))


def pack(ka, trials, spread, screened, parts):
    own = screened.shape[1] // parts
    half = own // 2

    def block(i):
        return pl.BlockSpec((1, own, own), lambda g, y: (0, (y[0] + i) % parts, y[0]))

    rows = trials.shape[1] // spread.shape[0] + 10 * half + 8
    return pl.pallas_call(
        pack_body,
        out_shape=jax.ShapeDtypeStruct((rows, half), F32),
        grid_spec=pltpu.PrefetchScalarGridSpec(
            num_scalar_prefetch=1,
            grid=(1,),
            in_specs=[
                pl.BlockSpec(trials.shape, lambda g, y: (0, 0)),
                pl.BlockSpec(spread.shape, lambda g, y: (0, 0)),
                block(0),
                block(1),
                block(2),
            ],
            out_specs=pl.BlockSpec((rows, half), lambda g, y: (0, 0)),
        ),
    )(ka, trials, spread, screened, screened, screened)


def prepare_body(ka_ref, *refs):
    parts = len(refs) // 3 - 1
    conduct_ref, conduct_next_ref, rows_ref, joined_ref = refs[3 * parts :]
    each, width = refs[0].shape[1:]
    for i in range(3):
        for k in range(parts):
            place = pl.multiple_of(lax.rem(ka_ref[0] + parts - k, parts) * each, each)
            high, low = split(refs[i * parts + k][0])
            rows_ref[0, pl.ds(place, each), i * width : (i + 1) * width] = high
            rows_ref[0, pl.ds(parts * each + place, each), i * width : (i + 1) * width] = low
    joined_ref[0, :, :width] = conduct_ref[0]
    joined_ref[0, :, width:] = conduct_next_ref[0].astype(BF16)


def prepare(ka, valence, conduction, conduction_next):
    pairs, rows, waves = valence[0].shape
    parts = len(valence)
    own = waves // parts
    columns = conduction.shape[1]

    def column(i):
        return pl.BlockSpec((1, rows, own), lambda p, y: (p, 0, (y[0] + i) % parts))

    conduct = pl.BlockSpec((1, columns, own), lambda p, y: (p, 0, 0))
    shapes = (pairs, 2 * parts * rows, 3 * own), (pairs, columns, 2 * own)
    return pl.pallas_call(
        prepare_body,
        out_shape=tuple(jax.ShapeDtypeStruct(shape, BF16) for shape in shapes),
        grid_spec=pltpu.PrefetchScalarGridSpec(
            num_scalar_prefetch=1,
            grid=(pairs,),
            in_specs=[column(i) for i in range(3) for _ in range(parts)] + [conduct, conduct],
            out_specs=tuple(pl.BlockSpec((1,) + shape[1:], lambda p, y: (p, 0, 0)) for shape in shapes),
        ),
        cost_estimate=pl.CostEstimate(flops=0, bytes_accessed=pairs * rows * waves * 40, transcendentals=0),
    )(ka, *(valence * 3), conduction, conduction_next)


def one_pair(rows, blocks, conduct, out_ref, low_ref, high_ref, skip):
    half = blocks.shape[1]
    width = 2 * half
    count = rows.shape[0] // 2
    squares = [blocks[skip + i * half : skip + (i + 1) * half] for i in range(10)]
    line = blocks[skip + 10 * half : skip + 10 * half + 1]
    row = lax.broadcasted_iota(jnp.int32, (half, half), 0)
    column = lax.broadcasted_iota(jnp.int32, (half, half), 1)
    shared, corner = squares[:2]
    turned = shared.T
    a = jnp.where(row <= column, shared, turned)
    d = jnp.where(row > column, shared, jnp.where(row == column, line, turned))
    left = jnp.concatenate([a, corner.T, squares[2], squares[4], squares[6], squares[8]], axis=0)
    right = jnp.concatenate([corner, d, squares[3], squares[5], squares[7], squares[9]], axis=0)
    high, low = split(jnp.concatenate([left, right], axis=1))
    both = mul(rows, high, PLAIN)
    here = both[:count] + both[count:] + mul(rows[:count], low, PLAIN)
    both = mul(rows[:, :width], high[width : 2 * width], TURNED)
    there = both[:count] + both[count:] + mul(rows[:count, :width], low[width : 2 * width], TURNED)
    high, low = split(jnp.concatenate([here, there], axis=1))
    both = mul(jnp.concatenate([high, low], axis=0), conduct, TURNED)
    kernel = both[:count] + both[count:]
    low_ref[...] = kernel[:, :VC]
    high_ref[...] = jnp.concatenate([kernel[:, VC:], jnp.zeros((count, 2 * VC - kernel.shape[1]), F32)], axis=1)
    group = lax.broadcasted_iota(jnp.int32, (VB, VC), 1) // CD
    for part, ref in enumerate((low_ref, high_ref)):
        tiles = [ref[pl.ds(w, VB, stride=VB), :] for w in range(VB)]
        for step in (4, 2, 1):
            upper = (group & step) != 0
            for i in range(VB):
                if i & step:
                    continue
                a, b = tiles[i], tiles[i + step]
                tiles[i] = jnp.where(upper, pltpu.roll(b, step * CD, axis=1), a)
                tiles[i + step] = jnp.where(upper, b, pltpu.roll(a, VC - step * CD, axis=1))
        for i in range(VB):
            c = part * VB + i
            if c < CB:
                out_ref[0, c * VB : (c + 1) * VB, :] = tiles[i]


def pair_body(skip, momentum_ref, rows_ref, *refs):
    blocks, conduct_ref, outs, scratch = refs[:PAIR], refs[PAIR], refs[PAIR + 1 : 2 * PAIR + 1], refs[2 * PAIR + 1 :]
    for i in range(PAIR):
        one_pair(rows_ref[i], blocks[i][0], conduct_ref[i], outs[i], scratch[2 * i], scratch[2 * i + 1], skip)


def pair_kernels(start, count, momentum, rows, blocks, conduct, skip):
    first = start // PAIR

    def block(i):
        return pl.BlockSpec((1,) + blocks.shape[1:], lambda p, q: (q[start + PAIR * p + i], 0, 0))

    return pl.pallas_call(
        lambda *refs: pair_body(skip, *refs),
        out_shape=[jax.ShapeDtypeStruct((count // PAIR, VB * CB, VC), F32)] * PAIR,
        grid_spec=pltpu.PrefetchScalarGridSpec(
            num_scalar_prefetch=1,
            grid=(count // PAIR,),
            in_specs=[pl.BlockSpec((PAIR,) + rows.shape[1:], lambda p, q: (first + p, 0, 0))]
            + [block(i) for i in range(PAIR)]
            + [pl.BlockSpec((PAIR,) + conduct.shape[1:], lambda p, q: (first + p, 0, 0))],
            out_specs=[pl.BlockSpec((1, VB * CB, VC), lambda p, q: (p, 0, 0))] * PAIR,
            scratch_shapes=[pltpu.VMEM((VB * VB, VC), F32)] * (2 * PAIR),
        ),
        cost_estimate=pl.CostEstimate(flops=count * 10**8, bytes_accessed=count * 11 * 10**5, transcendentals=0),
    )(momentum, rows, *([blocks] * PAIR), conduct)


def response_body(start, counts, near_ref, far_ref, near_place_ref, far_place_ref, trial_ref, *refs):
    kernels, (out_ref, turn_ref) = refs[: len(counts)], refs[-2:]
    last = len(refs) > len(counts) + 2
    if last:
        before_ref, first_ref, second_ref, turn_ref, out_ref = refs[len(counts) :]
        out_ref[...] = before_ref[...]
    else:
        out_ref[...] = jnp.zeros_like(out_ref)
    turn_ref[...] = jnp.zeros_like(turn_ref)
    for number, (count, kernel_ref) in enumerate(zip(counts, kernels)):

        @pl.loop(0, count)
        def _(p, number=number, kernel_ref=kernel_ref):
            pair = start + PAIR * p + number
            near, far = near_ref[pair], far_ref[pair]
            for v in range(VB):
                turn_ref[v * CD : v * CD + CB, :] = kernel_ref[p, pl.ds(v, CB, stride=VB), :]
            kernel = turn_ref[...]
            direct = mul3(trial_ref[far], kernel, TURNED)
            mirror = mul3(trial_ref[near], kernel, PLAIN)
            near, far = near_place_ref[pair], far_place_ref[pair]
            out_ref[near] = out_ref[near] + direct
            out_ref[far] = out_ref[far] + mirror

    if last:
        half = first_ref.shape[0]
        first_ref[...] = out_ref[:half]
        second_ref[...] = out_ref[half:]


def contributions(start, places, blocks, trials, kernels, before=()):
    counts = [kernel.shape[0] for kernel in kernels]
    shape = (blocks.shape[0], trials, VC)
    whole = [pl.BlockSpec(x.shape, lambda g: (0, 0, 0)) for x in kernels]
    shape_out = (shape[0] // (1 + len(before)),) + shape[1:]
    result = pl.BlockSpec(shape, lambda g: (0, 0, 0))
    scalar = pl.BlockSpec(memory_space=pltpu.SMEM)
    return pl.pallas_call(
        lambda *refs: response_body(start, counts, *refs),
        out_shape=[jax.ShapeDtypeStruct(shape_out, F32)] * (1 + len(before)),
        grid=(1,),
        in_specs=[scalar] * len(places) + [result, *whole] + [result] * len(before),
        out_specs=[pl.BlockSpec(shape_out, lambda g: (0, 0, 0))] * (1 + len(before)),
        scratch_shapes=[pltpu.VMEM((VC, VC), F32)] + [pltpu.VMEM(shape, F32)] * len(before),
        cost_estimate=pl.CostEstimate(flops=sum(counts) * 10**7, bytes_accessed=4 * 10**6, transcendentals=0),
    )(*places, blocks, *kernels, *before)


def compute(valence, conduction, screened, momentum, kpairs, kpoint_slot, trial_blocks):
    ka = lax.axis_size("ka")
    pair_dev = valence.shape[0]
    own = conduction.shape[2]
    here = lax.axis_index("ka").astype(jnp.int32).reshape(1)
    local_trials = trial_blocks.shape[1] // (VB * CB)
    entry = np.arange(VB * CB)
    spread = np.zeros((VB * CB, VC), np.float32)
    spread[entry, entry // CB * CD + entry % CB] = 1.0
    blocks = lax.all_gather(pack(here, trial_blocks, jnp.asarray(spread), screened, ka), "pb")

    ahead = [(i, (i + 1) % ka) for i in range(ka)]
    back = [((i + 1) % ka, i) for i in range(ka)]
    conduct = conduction.reshape(pair_dev, CB, CB, own)
    conduct = jnp.pad(conduct, ((0, 0), (0, 0), (0, CD - CB), (0, 0))).reshape(pair_dev, CB * CD, own)
    conduct_next = lax.ppermute(conduct.astype(F32), "ka", back)
    rows = [valence]
    for _ in range(ka - 1):
        rows.append(lax.ppermute(rows[-1], "ka", ahead))
    near = jnp.take(kpoint_slot, kpairs[:, 0])
    far = jnp.take(kpoint_slot, kpairs[:, 1])
    rows, conduct = prepare(here, rows, conduct, conduct_next)
    owners = lax.axis_size("pb")
    core = lax.rem(lax.axis_index("pb").astype(jnp.int32), 2)
    places = [near, far] + [lax.rem(x + core, 2) * (owners // 2) + x // 2 for x in (near, far)]
    rows, conduct, places = lax.optimization_barrier((rows, conduct, places))

    swap = [(i, i ^ 1) for i in range(ka)]
    fold = [(i, ka - 1 - i) for i in range(ka)]
    target = momentum[:, 0]
    turns = (swap, fold)
    cut = pair_dev * 5 // (8 * PAIR) * PAIR

    def exchanged(number, first):
        return [x + lax.ppermute(x, "ka", turns[(i + number) % 2]) for i, x in enumerate(first)]

    first = pair_kernels(0, cut, target, rows, blocks, conduct, local_trials)
    first = exchanged(0, first)
    second = pair_kernels(cut, pair_dev - cut, target, rows, blocks, conduct, local_trials)
    first = exchanged(1, first)
    second = exchanged(0, second)
    second = exchanged(1, second)
    (summed,) = contributions(0, places, blocks, local_trials, first)
    mine, other = contributions(cut, places, blocks, local_trials, second, (summed,))
    other = lax.ppermute(other, "pb", [(i, i ^ 1) for i in range(owners)])
    groups = [list(range(c, owners, 2)) for c in range(2)]
    parts = lax.all_to_all(mine + other, "pb", split_axis=0, concat_axis=0, axis_index_groups=groups, tiled=True)
    response = jnp.sum(parts, axis=0).reshape(local_trials, VB, CD)[:, :, :CB]
    return response.reshape(1, -1)


def solution(mesh):
    return jax.shard_map(
        compute,
        mesh=mesh,
        in_specs=(
            P("pb", "ka", None),
            P("pb", None, "ka"),
            P("pb", None, None),
            P("pb", None),
            P("pb", None),
            P(),
            P("pb", "ka"),
        ),
        out_specs=P("pb", "ka"),
        check_vma=False,
    )
```
